32 devices in a mesh: wide: 8 (over z, x), narrow: 4 (over y, core).
Axes of the slice: x: 2, y: 2, z: 4, core: 2. Of those that a mesh axis runs over, the one named last changes fastest.
Arguments:
- pressure: float32 [1024, 128], P(('wide', 'narrow')), may hold values from -6 to 6
- right_side: float32 [1024, 128], P(('wide', 'narrow')), may hold values from -6 to 6
- concentration: float32 [1024, 128], P(('wide', 'narrow')), may hold values from 0 to 1
- pore_volume: float32 [1024, 128], P(('wide', 'narrow')), may hold values from 0.5 to 2
- well_rate: float32 [1024, 128], P(('wide', 'narrow')), may hold values from 0.02 to 0.5
- inject_conc: float32 [1024, 128], P(('wide', 'narrow')), may hold values from 0 to 1
- transmissibility: float32 [6, 131072], P(None, ('wide', 'narrow')), may hold values from 0.1 to 1
- face_neighbor: int32 [6, 1024], P(None, ('wide', 'narrow')), may hold values from 0 to 56, as said below
- sub_matrix: bfloat16 [2048, 4, 128, 128], P(('wide', 'narrow')), as said below
- sub_columns: int32 [2048, 4], P(('wide', 'narrow')), may hold values from 0 to 63, as said below
- send_blocks: int32 [32, 4, 8], P(('wide', 'narrow')), may hold values from 0 to 31, as said below
- send_counts: int32 [32, 4], P(('wide', 'narrow')), may hold values from 1 to 8, as said below
- basis_weights: bfloat16 [8192, 4096], P(('wide', 'narrow')), may hold values from -0.09375 to 0.09375
- coarse_index: int32 [8192], P(('wide', 'narrow')), may hold values from 0 to 4095, as said below
- coarse_inverse: float32 [4096, 512], P(('wide', 'narrow')), may hold values from -0.25 to 0.25
Outputs:
- pressure_new: float32 [1024, 128], P(('wide', 'narrow'))
- concentration_new: float32 [1024, 128], P(('wide', 'narrow'))
The draws below stay inside these ranges and needn't reach their ends.
Inputs may be any that keep to these rules, and one draw needn't show every extreme that they name: `send_blocks`: local block indices below 32. `send_counts`: between 1 and 8; the first subdomain sends 8 blocks to every neighbour and the last sends one. `sub_columns`: slot 0 of each row block names the row block itself. `face_neighbor`: each owned block's faces name owned blocks or the first received block from some neighbour. `coarse_index`: a subdomain's functions may be owned by any index of wide, and may repeat. `sub_matrix`: the diagonal of each row block's first stored block lies between 0.9 and 2.1.
All inputs are finite; a program needn't handle non-finite values.
Results may differ from the reference program's by a relative error of at most 0.00225.
The reference program's roundings to bfloat16 on the way (of `pressure_b`, `residual_b` and `coarse_b`) count: a program that leaves them out, or rounds other values in their place, can miss the bound.
Values may be sent and summed in bfloat16 or wider, within the bound.
A program may use at most 64 MiB of HBM per device.

```python
import math
import jax
import jax.numpy as jnp
from jax import lax

BS = 128
BD = 32
SL = 8
EXT = 64
EROWS = 2048
NNZB = 4
SWEEPS = 4
NFACE = 6
NCL = 256
NCO = 512
NC = 4096
BLOCKS = 1024
CELLS = 131072
N_WIDE = 8
N_NARROW = 4
DEVICES = 32


def draw_sub_matrix(key, part):
    noise_key, diag_key = jax.random.split(key)
    noise = jax.random.normal(noise_key, (EROWS, NNZB, BS, BS), jnp.float32) * (0.3 / math.sqrt(NNZB * BS))
    diag_values = jax.random.uniform(diag_key, (EROWS, 1, BS, 1), jnp.float32, 1.0, 2.0)
    first_slot = (jnp.arange(NNZB) == 0).astype(jnp.float32)[None, :, None, None]
    identity = jnp.eye(BS, dtype=jnp.float32)[None, None]
    return (noise + first_slot * identity * diag_values).astype(jnp.bfloat16)


def draw_sub_columns(key, part):
    own_rows = (jnp.arange(EROWS, dtype=jnp.int32) % EXT)[:, None]
    others = jax.random.randint(key, (EROWS, NNZB - 1), 0, EXT, dtype=jnp.int32)
    return jnp.concatenate([own_rows, others], axis=1)


def draw_send_blocks(key, part):
    return jax.random.randint(key, (DEVICES, 4, SL), 0, BD, dtype=jnp.int32)


def draw_send_counts(key, part):
    counts = jax.random.randint(key, (DEVICES, 4), 1, SL + 1, dtype=jnp.int32)
    counts = counts.at[0].set(SL)
    return counts.at[DEVICES - 1].set(1)


def draw_coarse_index(key, part):
    return jax.random.randint(key, (DEVICES * NCL,), 0, NC, dtype=jnp.int32)


def draw_face_neighbor(key, part):
    first_key, second_key = jax.random.split(key)
    block_local = jnp.arange(BLOCKS, dtype=jnp.int32) % BD
    turn = jax.random.randint(first_key, (), 0, 4, dtype=jnp.int32)
    direction = (jnp.arange(BLOCKS, dtype=jnp.int32) + turn) % 4
    margin_block = BD + direction * SL
    random_block = jax.random.randint(second_key, (BLOCKS,), 0, BD, dtype=jnp.int32)
    return jnp.stack([(block_local + 1) % BD, (block_local - 1) % BD, (block_local + 2) % BD, (block_local - 2) % BD, margin_block, random_block], axis=0)


def levels(own_key, dims, shards, least, top_value):
    loudness, own = 1.0, jax.random.fold_in(own_key, 6)
    for axis_at, parts in shards:
        steps = jnp.exp(jax.random.uniform(jax.random.fold_in(own, axis_at), (parts,), jnp.float32, least / len(shards), top_value / len(shards)))
        loudness = loudness * jnp.repeat(steps, dims[axis_at] // parts).reshape([-1 if axis == axis_at else 1 for axis in range(len(dims))])
    return loudness


def centred(rng, extent, scale, reach, cuts=(), kind=jnp.bfloat16):
    level = levels(rng, extent, cuts, -0.22, 0.18) if cuts else 1.0
    entries = jax.random.normal(rng, extent, jnp.float32) * scale * level
    return jnp.minimum(jnp.maximum(entries, -reach), reach).astype(kind)


def setup_inputs(seed: int = 0) -> dict:
    streams_of = jax.random.split(jax.random.key(seed), 16)
    pressure = centred(streams_of[0], (BLOCKS, BS), 1.0, 6.0, ((0, 32),), jnp.float32)
    right_side = centred(streams_of[1], (BLOCKS, BS), 1.0, 6.0, ((0, 32),), jnp.float32)
    concentration = jnp.clip(1.0 * jax.random.uniform(streams_of[2], (BLOCKS, BS), jnp.float32) ** levels(streams_of[2], (BLOCKS, BS), ((0, 32),), -0.2, 0.2), 0.0, 1.0)
    pore_volume = jnp.clip(jnp.exp(math.log(2.0) - 1.3862944 * jax.random.uniform(streams_of[3], (BLOCKS, BS), jnp.float32) ** levels(streams_of[3], (BLOCKS, BS), ((0, 32),), -0.2, 0.2)), 0.5, 2.0)
    well_rate = jnp.clip(jnp.exp(math.log(0.5) - 3.218876 * jax.random.uniform(streams_of[4], (BLOCKS, BS), jnp.float32) ** levels(streams_of[4], (BLOCKS, BS), ((0, 32),), -0.2, 0.2)), 0.02, 0.5)
    inject_conc = jnp.clip(1.0 * jax.random.uniform(streams_of[5], (BLOCKS, BS), jnp.float32) ** levels(streams_of[5], (BLOCKS, BS), ((0, 32),), -0.2, 0.2), 0.0, 1.0)
    transmissibility = jnp.clip(jnp.exp(math.log(1.0) - 2.3025851 * jax.random.uniform(streams_of[6], (NFACE, CELLS), jnp.float32) ** levels(streams_of[6], (NFACE, CELLS), ((1, 32),), -0.2, 0.2)), 0.1, 1.0)
    face_neighbor = draw_face_neighbor(jax.random.fold_in(streams_of[15], 71), 0)
    sub_matrix = draw_sub_matrix(jax.random.fold_in(streams_of[15], 71), 0)
    sub_columns = draw_sub_columns(jax.random.fold_in(streams_of[15], 71), 0)
    send_blocks = draw_send_blocks(jax.random.fold_in(streams_of[15], 71), 0)
    send_counts = draw_send_counts(jax.random.fold_in(streams_of[15], 71), 0)
    basis_weights = centred(streams_of[12], (DEVICES * NCL, BD * BS), (BD * BS) ** -0.5, 0.09375, ((0, 32),))
    coarse_index = draw_coarse_index(jax.random.fold_in(streams_of[15], 71), 0)
    coarse_inverse = centred(streams_of[14], (NC, NCO), NCO ** -0.5, 0.25, ((0, 32),), jnp.float32)
    return dict(pressure=pressure, right_side=right_side, concentration=concentration, pore_volume=pore_volume, well_rate=well_rate, inject_conc=inject_conc, transmissibility=transmissibility, face_neighbor=face_neighbor, sub_matrix=sub_matrix, sub_columns=sub_columns, send_blocks=send_blocks, send_counts=send_counts, basis_weights=basis_weights, coarse_index=coarse_index, coarse_inverse=coarse_inverse)


shift_offsets = (2, 1, -1, -2)
courant = 0.9


def product_ref(matrix, columns, vector_b):
    vector_b = lax.optimization_barrier(vector_b)
    picked = vector_b[columns].astype(jnp.float32)
    return jnp.einsum("rkij,rkj->ri", matrix.astype(jnp.float32), picked)


def outgoing(owned_rows, send_blocks, send_counts):
    slot_count = send_blocks.shape[-1]
    active = jnp.arange(slot_count)[None, None, :] < send_counts[:, :, None]
    picked = jax.vmap(lambda block_rows, chosen: block_rows[chosen])(owned_rows, send_blocks)
    return jnp.where(active[..., None], picked, jnp.zeros_like(picked))


def extended(owned_rows, send_blocks, send_counts, wide_count):
    packed = outgoing(owned_rows, send_blocks, send_counts)
    devices = owned_rows.shape[0]
    narrow_count = devices // wide_count
    slot_count = send_blocks.shape[-1]
    grid = packed.reshape((wide_count, narrow_count) + packed.shape[1:])
    collected = [owned_rows]
    for position, offset in enumerate(shift_offsets):
        source = grid[:, :, position]
        zero_rows = jnp.zeros((abs(offset),) + source.shape[1:], source.dtype)
        if offset > 0:
            moved_rows = jnp.concatenate([zero_rows, source[:wide_count - offset]], axis=0)
        else:
            moved_rows = jnp.concatenate([source[-offset:], zero_rows], axis=0)
        collected.append(moved_rows.reshape((devices, slot_count) + source.shape[3:]))
    return jnp.concatenate(collected, axis=1)


def reference(pressure, right_side, concentration, pore_volume, well_rate, inject_conc, transmissibility, face_neighbor, sub_matrix, sub_columns, send_blocks, send_counts, basis_weights, coarse_index, coarse_inverse):
    wide_count = N_WIDE
    devices = N_WIDE * N_NARROW
    cells_dev = BD * BS
    pressure_dev = pressure.reshape(devices, BD, BS)
    right_dev = right_side.reshape(devices, BD, BS)
    conc_dev = concentration.reshape(devices, BD, BS)
    matrix_dev = sub_matrix.reshape(devices, EXT, NNZB, BS, BS)
    columns_dev = sub_columns.reshape(devices, EXT, NNZB)
    pressure_b = pressure_dev.astype(jnp.bfloat16)
    ext_pressure = extended(pressure_b, send_blocks, send_counts, wide_count)

    def residual_one(members):
        matrix, columns, ext_vector, right_rows = members
        return right_rows - product_ref(matrix[:BD], columns[:BD], ext_vector)

    residual = lax.map(residual_one, (matrix_dev, columns_dev, ext_pressure, right_dev))
    residual_b = residual.astype(jnp.bfloat16)
    ext_residual = extended(residual_b, send_blocks, send_counts, wide_count)

    def smooth_one(members):
        matrix, columns, ext_vector = members
        diagonal = jnp.diagonal(matrix[:, 0], axis1=1, axis2=2).astype(jnp.float32)
        target = ext_vector.astype(jnp.float32)
        update = jnp.zeros(target.shape, jnp.float32)
        for turn_index in range(SWEEPS):
            update = update + (target - product_ref(matrix, columns, update.astype(jnp.bfloat16))) / diagonal
        return update[:BD]

    local_update = lax.map(smooth_one, (matrix_dev, columns_dev, ext_residual))
    basis_dev = basis_weights.reshape(devices, NCL, cells_dev)
    local_coarse = lax.map(lambda members: jnp.dot(members[0], members[1].reshape(-1), preferred_element_type=jnp.float32), (basis_dev, residual_b))
    coarse_residual = jnp.zeros((NC,), jnp.float32).at[coarse_index].add(local_coarse.reshape(-1))
    inverse_blocks = coarse_inverse.reshape(N_WIDE, NCO, NCO)
    coarse_values = jnp.einsum("wij,wj->wi", inverse_blocks, coarse_residual.reshape(N_WIDE, NCO), precision=lax.Precision.HIGHEST).reshape(-1)
    coarse_b = coarse_values.astype(jnp.bfloat16)
    index_dev = coarse_index.reshape(devices, NCL)
    correction = lax.map(lambda members: jnp.dot(coarse_b[members[1]], members[0], preferred_element_type=jnp.float32), (basis_dev, index_dev))
    pressure_next = pressure_dev + local_update + correction.reshape(devices, BD, BS)
    ext_next = extended(pressure_next, send_blocks, send_counts, wide_count)
    ext_conc = extended(conc_dev, send_blocks, send_counts, wide_count)
    neighbor_dev = face_neighbor.reshape(NFACE, devices, BD).transpose(1, 0, 2)
    trans_dev = transmissibility.reshape(NFACE, devices, cells_dev).transpose(1, 0, 2)
    near_pressure = jax.vmap(lambda values, where_to: values[where_to])(ext_next, neighbor_dev).reshape(devices, NFACE, cells_dev)
    near_conc = jax.vmap(lambda values, where_to: values[where_to])(ext_conc, neighbor_dev).reshape(devices, NFACE, cells_dev)
    own_pressure = pressure_next.reshape(devices, 1, cells_dev)
    own_conc = conc_dev.reshape(devices, 1, cells_dev)
    face_flux = trans_dev * (own_pressure - near_pressure)
    outward = jnp.maximum(face_flux, 0.0)
    inward = jnp.minimum(face_flux, 0.0)
    advection = jnp.sum(outward * own_conc + inward * near_conc, axis=1)
    outflow = jnp.sum(outward, axis=1)
    volume_flat = pore_volume.reshape(devices, cells_dev)
    rate_flat = well_rate.reshape(devices, cells_dev)
    cell_rate = (outflow + rate_flat) / volume_flat
    time_step = courant / jnp.max(cell_rate)
    conc_flat = conc_dev.reshape(devices, cells_dev)
    inject_flat = inject_conc.reshape(devices, cells_dev)
    conc_next = conc_flat + time_step / volume_flat * (rate_flat * (inject_flat - conc_flat) - advection)
    return pressure_next.reshape(BLOCKS, BS), conc_next.reshape(BLOCKS, BS)
```

```python
import functools

import jax
import jax.numpy as jnp
from jax import lax
from jax.experimental import pallas as pl
from jax.experimental.pallas import tpu as pltpu
from jax.sharding import PartitionSpec as P

SWEEPS = 4

shift_offsets = (2, 1, -1, -2)
courant = 0.9
MESH = pl.DeviceIdType.MESH
f32, bf16 = jnp.float32, jnp.bfloat16
contract_last = (((1,), (1,)), ((), ()))
plain = (((1,), (0,)), ((), ()))
PRESSURE, RESIDUAL, EXTRAS, BASIS, UPDATE = range(5)


def rounded(value):
    return value.astype(bf16).astype(f32)


def kernel(
    wide_count,
    narrow_count,
    face_hbm,
    columns_hbm,
    blocks_hbm,
    counts_hbm,
    index_hbm,
    pressure_hbm,
    right_hbm,
    conc_hbm,
    volume_hbm,
    rate_hbm,
    inject_hbm,
    trans_hbm,
    matrix_hbm,
    basis_hbm,
    inverse_hbm,
    pressure_out,
    conc_out,
    face_neighbor,
    sub_columns,
    send_blocks,
    send_counts,
    index_row,
    pressure,
    right_side,
    conc,
    volume,
    rate,
    inject,
    trans,
    matrix,
    basis,
    inverse,
    load_sem,
    outbox,
    inbox,
    extras_out,
    extras_in,
    basis_out,
    basis_in,
    update_out,
    update_in,
    margin_send,
    margin_recv,
    own,
    ext_a,
    ext_b,
    target,
    diag,
    picked,
    row_of,
    lane_of,
    partial,
    residual_in,
    value_in,
    value_mine,
    top_mine,
    top_in,
    all_send,
    all_recv,
    near_p,
    near_c,
    ext_c,
    adv,
    grow,
):
    w, n = lax.axis_index("wide"), lax.axis_index("narrow")
    devices, me = wide_count * narrow_count, w * narrow_count + n
    owned, lanes = pressure.shape
    extent = ext_a.shape[0]
    slots = outbox.shape[2]
    faces = trans.shape[0]
    functions = index_row.shape[1]
    chunks = functions // lanes
    groups = partial.shape[1]
    coarse_rows, coarse_width = inverse.shape
    coarse_lines = wide_count * groups

    def wrapped(at, count):
        return jnp.where(at >= count, at - count, at)

    def inside(offset):
        return jnp.logical_and(w + offset >= 0, w + offset < wide_count)

    def others_narrow(body):
        for step in range(1, narrow_count):
            body(w, wrapped(n + step, narrow_count))

    def signal(sem, row, column):
        pl.semaphore_signal(sem, inc=1, device_id=(row, column), device_id_type=MESH)

    barrier = pltpu.get_barrier_semaphore()

    def meet(sem, offsets):
        for offset in offsets:
            @pl.when(inside(offset))
            def _():
                signal(sem, w + offset, n)

    def met(sem, offsets, more=0):
        pl.semaphore_wait(sem, more + sum(jnp.where(inside(offset), 1, 0) for offset in offsets))

    meet(barrier, shift_offsets)
    others_narrow(lambda row, column: signal(barrier, row, column))

    loads = {}

    def load(name, source, place):
        copy = pltpu.make_async_copy(source, place, load_sem.at[len(loads)])
        copy.start()
        loads[name] = copy

    def ready(*names):
        for name in names:
            loads[name].wait()

    rest = extent - owned
    load("pressure", pressure_hbm, pressure)
    load("blocks", blocks_hbm, send_blocks)
    load("counts", counts_hbm, send_counts)
    load("columns", columns_hbm, sub_columns)
    load("index", index_hbm, index_row)
    load("matrix", matrix_hbm.at[pl.ds(0, owned)], matrix.at[pl.ds(0, owned)])
    load("right", right_hbm, right_side)
    load("conc", conc_hbm, conc)
    load("basis", basis_hbm, basis)
    load("more", matrix_hbm.at[pl.ds(owned, rest)], matrix.at[pl.ds(owned, rest)])
    load("inverse", inverse_hbm, inverse)
    load("faces", face_hbm, face_neighbor)
    load("trans", trans_hbm, trans)
    load("volume", volume_hbm, volume)
    load("rate", rate_hbm, rate)
    load("inject", inject_hbm, inject)

    boxes = (
        lambda at: (outbox.at[0, at], inbox.at[0, at]),
        lambda at: (outbox.at[1, at], inbox.at[1, at]),
        lambda at: (extras_out.at[at], extras_in.at[at]),
        lambda at: (basis_out.at[at], basis_in.at[at]),
        lambda at: (update_out.at[at], update_in.at[at]),
    )

    def margin_copy(kind, position):
        source, place = boxes[kind](position)
        return pltpu.make_async_remote_copy(
            src_ref=source,
            dst_ref=place,
            send_sem=margin_send.at[kind, position],
            recv_sem=margin_recv.at[kind, position],
            device_id=(w + shift_offsets[position], n),
            device_id_type=MESH,
        )

    slot_id = lax.broadcasted_iota(jnp.int32, (slots, lanes), 0)

    def pack(turn, rows):
        for position in range(4):
            for t in range(slots):
                outbox[turn, position, pl.ds(t, 1), :] = rows[pl.ds(send_blocks[0, position, t], 1), :]
            filled = outbox[turn, position]
            outbox[turn, position] = jnp.where(slot_id < send_counts[0, position], filled, 0.0)

    def send_margin(kind):
        for position, offset in enumerate(shift_offsets):
            @pl.when(inside(offset))
            def _():
                margin_copy(kind, position).start()

    def take_margin(kind, use, nothing):
        for position, offset in enumerate(shift_offsets):
            @pl.when(inside(-offset))
            def _():
                margin_copy(kind, position).wait_recv()
                use(position)

            @pl.when(jnp.logical_not(inside(-offset)))
            def _():
                nothing(position)

    def take_rows(turn, place):
        def use(position):
            place[pl.ds(owned + position * slots, slots), :] = inbox[turn, position]

        def nothing(position):
            place[pl.ds(owned + position * slots, slots), :] = jnp.zeros((slots, lanes), f32)

        take_margin(turn, use, nothing)

    def exchange(turn, send_from, land_in):
        def start():
            def send(row, column):
                pltpu.make_async_remote_copy(
                    src_ref=send_from(row),
                    dst_ref=land_in.at[me],
                    send_sem=all_send.at[turn],
                    recv_sem=all_recv.at[turn],
                    device_id=(row, column),
                    device_id_type=MESH,
                ).start()

            columns = [n] + [wrapped(n + step, narrow_count) for step in range(1, narrow_count)]

            @pl.loop(1, wide_count)
            def _(step):
                row = wrapped(w + step, wide_count)
                for column in columns:
                    send(row, column)

            others_narrow(send)

        others = land_in.at[pl.ds(0, devices - 1)]
        every = pltpu.make_async_remote_copy(
            src_ref=others,
            dst_ref=others,
            send_sem=all_send.at[turn],
            recv_sem=all_recv.at[turn],
            device_id=(wrapped(w + 1, wide_count), n),
            device_id_type=MESH,
        )
        return start, every.wait_recv, every.wait_send

    residuals = exchange(0, lambda row: partial.at[row], residual_in)
    values_all = exchange(1, lambda row: value_mine, value_in)
    tops = exchange(2, lambda row: top_mine, top_in)

    ready("pressure", "blocks", "counts")
    own[...] = rounded(pressure[...])
    pack(0, own)
    met(barrier, shift_offsets, narrow_count - 1)
    send_margin(PRESSURE)

    radius, rounds = 2, []
    while radius < wide_count - 1:
        rounds.append((radius, -radius))
        radius *= 2
    if rounds:
        meet(grow.at[0], rounds[0])

    ready("index")
    power = coarse_rows.bit_length() - 1

    def spread_index(part, line, place):
        tall = jnp.broadcast_to(line, (lanes, lanes)).T.astype(jnp.int32)
        rows = pl.ds(part * lanes, lanes)
        line_of = jnp.right_shift(tall, power)
        wide_id = lax.broadcasted_iota(jnp.int32, (lanes, devices), 1)
        row_of[rows, :] = jnp.where(line_of[:, :1] == wide_id, 1.0, 0.0).astype(bf16)
        lane_of[rows, :] = jnp.bitwise_and(tall, coarse_rows - 1)
        return tall

    number = index_row[...]
    number_f = number.astype(f32)
    tall_parts = [spread_index(c, number_f[:, c * lanes : (c + 1) * lanes], None) for c in range(chunks)]
    lane_id = lax.broadcasted_iota(jnp.int32, (functions, lanes), 1)
    line_hot = jnp.where(
        jnp.right_shift(number, 7) == lax.broadcasted_iota(jnp.int32, (coarse_lines, functions), 0), 1.0, 0.0
    ).astype(bf16)

    for at, offsets in enumerate(rounds):
        met(grow.at[at], offsets)
        if at + 1 < len(rounds):
            meet(grow.at[at + 1], rounds[at + 1])
    last = grow.at[len(rounds)]
    others_narrow(lambda row, column: signal(last, row, column))

    ready("conc", "basis")
    for position in range(4):
        block = send_blocks[0, position, 0]
        extras_out[position, pl.ds(0, 1), :] = conc[pl.ds(block, 1), :]
        for c in range(chunks):
            extras_out[position, pl.ds(1 + c, 1), :] = number_f[:, c * lanes : (c + 1) * lanes]
        extras_out[position, pl.ds(1 + chunks, slots - 1 - chunks), :] = jnp.zeros((slots - 1 - chunks, lanes), f32)
        basis_out[position] = basis[:, pl.ds(block * lanes, lanes)]
    send_margin(EXTRAS)
    send_margin(BASIS)

    ready("matrix")
    eye = lax.broadcasted_iota(jnp.int32, (lanes, lanes), 0) == lax.broadcasted_iota(jnp.int32, (lanes, lanes), 1)

    def diagonals(start, stop):
        @pl.loop(start, stop, unroll=4)
        def _(row):
            block = matrix[row, 0].astype(f32)
            diag[pl.ds(row, 1), :] = jnp.sum(jnp.where(eye, block, 0.0), axis=0, keepdims=True)

    diagonals(0, owned)
    ready("columns", "right")

    sub_id = lax.broadcasted_iota(jnp.int32, (8, lanes), 0)

    def multiply(left, pairs):
        total = jnp.zeros((8, lanes), f32)
        for i, pair in pairs:
            blocks = jnp.concatenate([pair[:, k].reshape(2 * lanes, lanes) for k in range(4)], axis=1)
            made = lax.dot_general(left, blocks, contract_last, preferred_element_type=f32)
            total = jnp.where(sub_id == i, made[:, :lanes], total)
            total = jnp.where(sub_id == i + 1, made[:, lanes:], total)
        return total

    def pick(base, vector):
        for i in range(8):
            for k in range(4):
                picked[k, pl.ds(base + i, 1), :] = vector[pl.ds(sub_columns[k, base + i], 1), :]

    def product(group, vector):
        base = pl.multiple_of(group * 8, 8)
        if vector is not None:
            pick(base, vector)
        left = jnp.concatenate([picked[k, pl.ds(base, 8), :].astype(bf16) for k in range(4)], axis=1)
        return multiply(left, ((i, matrix[pl.ds(base + i, 2)]) for i in range(0, 8, 2)))

    def groups_of(count, body):
        @pl.loop(0, count // 8, unroll=2)
        def _(group):
            body(group, pl.ds(pl.multiple_of(group * 8, 8), 8))

    ext_a[pl.ds(0, owned), :] = own[...]
    take_rows(PRESSURE, ext_a)

    def residual_group(group, rows):
        own[rows, :] = rounded(right_side[rows, :] - product(group, ext_a))

    groups_of(owned, residual_group)
    pack(1, own)
    send_margin(RESIDUAL)

    flat = jnp.concatenate([own[pl.ds(b, 1), :] for b in range(owned)], axis=1)
    flat = jnp.broadcast_to(flat, (8, flat.shape[1])).astype(bf16)
    local_coarse = lax.dot_general(flat, basis[...], contract_last, preferred_element_type=f32)[0:1, :]
    tall_coarse = jnp.concatenate(
        [jnp.broadcast_to(local_coarse[:, c * lanes : (c + 1) * lanes], (lanes, lanes)).T for c in range(chunks)], axis=0
    )
    tall_index = jnp.concatenate(tall_parts, axis=0)
    placed = jnp.where(jnp.bitwise_and(tall_index, lanes - 1) == lane_id, tall_coarse, 0.0)
    high = placed.astype(bf16)
    left_over = placed - high.astype(f32)
    middle = left_over.astype(bf16)
    low = (left_over - middle.astype(f32)).astype(bf16)
    spread = lax.dot_general(
        line_hot, jnp.concatenate([high, middle, low], axis=1), plain, preferred_element_type=f32
    )
    spread = spread[:, :lanes] + spread[:, lanes : 2 * lanes] + spread[:, 2 * lanes :]
    for block in range(wide_count):
        partial[block] = spread[block * groups : (block + 1) * groups]
    pl.semaphore_wait(last, narrow_count - 1)
    residuals[0]()

    ready("more")
    diagonals(owned, extent)
    target[pl.ds(0, owned), :] = own[...]

    def use_extras(position):
        ext_c[pl.ds(owned + position * slots, slots), :] = extras_in[position]

    def no_extras(position):
        ext_c[pl.ds(owned + position * slots, slots), :] = jnp.zeros((slots, lanes), f32)
        basis_in[position] = jnp.zeros((functions, lanes), bf16)
        update_in[position] = jnp.zeros((1, lanes), f32)

    take_rows(RESIDUAL, target)
    ext_a[...] = target[...] / diag[...]

    def sweep(count, old, new, source):
        def body(group, rows):
            new[rows, :] = old[rows, :] + (target[rows, :] - product(group, source)) / diag[rows, :]

        groups_of(count, body)

    sweep(extent, ext_a, ext_b, ext_a)

    ready("inverse")
    residual_in[me] = partial[w]
    residuals[1]()
    block_sum = jnp.sum(residual_in[...], axis=0)
    weighed = inverse[:, :lanes] * block_sum[0:1]
    for c in range(1, groups):
        weighed += inverse[:, c * lanes : (c + 1) * lanes] * block_sum[c : c + 1]
    value_mine[...] = rounded(jnp.sum(weighed.T, axis=0, keepdims=True))
    value_in[me] = value_mine[...]
    values_all[0]()

    sweep(extent, ext_b, ext_a, ext_b)

    firsts = [send_blocks[0, position, 0] for position in range(4)]

    @pl.loop(0, owned // 8, unroll=2)
    def _(group):
        pick(pl.multiple_of(group * 8, 8), ext_a)

    left = jnp.concatenate(
        [
            jnp.concatenate([picked[k, pl.ds(firsts[position % 4], 1), :] for position in range(8)], axis=0).astype(bf16)
            for k in range(4)
        ],
        axis=1,
    )
    made = multiply(
        left,
        (
            (i, jnp.concatenate([matrix[pl.ds(firsts[i], 1)], matrix[pl.ds(firsts[i + 1], 1)]], axis=0))
            for i in range(0, 4, 2)
        ),
    )
    for position, block in enumerate(firsts):
        row = pl.ds(block, 1)
        change = (target[row, :] - made[position : position + 1]) / diag[row, :]
        update_out[position] = pressure[row, :] + (ext_a[row, :] + change)
    send_margin(UPDATE)

    sweep(owned, ext_a, ext_b, None)
    own[...] = pressure[...] + ext_b[pl.ds(0, owned), :]

    ext_c[pl.ds(0, owned), :] = conc[...]
    take_margin(EXTRAS, use_extras, no_extras)
    for position in range(4):
        for c in range(chunks):
            line = ext_c[pl.ds(owned + position * slots + 1 + c, 1), :]
            spread_index((1 + position) * chunks + c, line, None)

    def gather_faces(place, field):
        @pl.loop(0, owned, unroll=4)
        def _(b):
            for f in range(faces):
                place[b, pl.ds(f, 1), :] = field[pl.ds(face_neighbor[f, b], 1), :]

    ready("faces")
    gather_faces(near_c, ext_c)
    ready("trans", "volume", "rate", "inject")
    take_margin(BASIS, lambda position: None, lambda position: None)
    target[pl.ds(owned, extent - owned), :] = jnp.zeros((extent - owned, lanes), f32)

    values_all[1]()
    coarse = value_in[...].reshape(devices, coarse_rows).astype(bf16)
    lined = lax.dot_general(row_of[...], coarse, plain, preferred_element_type=f32)
    value_lane = lax.broadcasted_iota(jnp.int32, lined.shape, 1)
    lined = jnp.where(lane_of[:, :coarse_rows] == value_lane, lined, 0.0).astype(bf16)
    chosen = lax.dot_general(
        jnp.ones((8, coarse_rows), bf16), lined, contract_last, preferred_element_type=f32
    ).astype(bf16)
    correction = lax.dot_general(chosen[:, :functions], basis[...], plain, preferred_element_type=f32)
    near = [
        lax.dot_general(
            chosen[:, (1 + position) * functions : (2 + position) * functions],
            basis_in[position],
            plain,
            preferred_element_type=f32,
        )
        for position in range(4)
    ]
    for b in range(owned):
        target[pl.ds(b, 1), :] = own[pl.ds(b, 1), :] + correction[0:1, b * lanes : (b + 1) * lanes]
    take_margin(UPDATE, lambda position: None, lambda position: None)
    for position in range(4):
        target[pl.ds(owned + position * slots, 1), :] = update_in[position] + near[position][0:1]
    pressure_out[...] = target[pl.ds(0, owned), :]
    gather_faces(near_p, target)

    @pl.loop(0, owned, unroll=4)
    def _(b):
        row = pl.ds(b, 1)
        flux = trans[:, pl.ds(pl.multiple_of(b * lanes, lanes), lanes)] * (target[row, :] - near_p[b])
        outward, inward = jnp.maximum(flux, 0.0), jnp.minimum(flux, 0.0)
        adv[row, :] = jnp.sum(outward * conc[row, :] + inward * near_c[b], axis=0, keepdims=True)
        ext_b[row, :] = jnp.sum(outward, axis=0, keepdims=True)

    cell_rate = (ext_b[pl.ds(0, owned), :] + rate[...]) / volume[...]
    top_mine[...] = jnp.max(cell_rate, axis=0, keepdims=True)
    tops[0]()
    scaled = (rate[...] * (inject[...] - conc[...]) - adv[...]) / volume[...]

    for kind in range(5):
        for position, offset in enumerate(shift_offsets):
            @pl.when(inside(offset))
            def _():
                margin_copy(kind, position).wait_send()
    residuals[2]()
    values_all[2]()
    top_in[me] = top_mine[...]
    tops[1]()
    top = jnp.max(top_in[...], axis=0)
    time_step = courant / jnp.max(top, axis=1, keepdims=True)
    conc_out[...] = conc[...] + time_step * scaled
    tops[2]()


def hand_over(pressure, conc, pressure_out, conc_out, sem):
    copies = [
        pltpu.make_async_copy(pressure, pressure_out, sem.at[0]),
        pltpu.make_async_copy(conc, conc_out, sem.at[1]),
    ]
    for copy in copies:
        copy.start()
    for copy in copies:
        copy.wait()


def solution(mesh):
    wide_count, narrow_count = mesh.shape["wide"], mesh.shape["narrow"]

    def local(
        pressure,
        right_side,
        concentration,
        pore_volume,
        well_rate,
        inject_conc,
        transmissibility,
        face_neighbor,
        sub_matrix,
        sub_columns,
        send_blocks,
        send_counts,
        basis_weights,
        coarse_index,
        coarse_inverse,
    ):
        owned, lanes = pressure.shape
        extent = sub_matrix.shape[0]
        slots = send_blocks.shape[-1]
        faces = face_neighbor.shape[0]
        functions = coarse_index.shape[0]
        coarse_rows, coarse_width = coarse_inverse.shape
        devices = wide_count * narrow_count
        groups = coarse_width // lanes
        numbers = (face_neighbor, sub_columns.T, send_blocks, send_counts)
        index_row = coarse_index.reshape(1, functions)
        streamed = (
            pressure,
            right_side,
            concentration,
            pore_volume,
            well_rate,
            inject_conc,
            transmissibility,
            sub_matrix,
            basis_weights,
            coarse_inverse,
        )
        dma, vmem = pltpu.SemaphoreType.DMA, pltpu.VMEM
        field, ext = vmem((owned, lanes), f32), vmem((extent, lanes), f32)
        results = pl.pallas_call(
            functools.partial(kernel, wide_count, narrow_count),
            out_shape=(vmem((owned, lanes), f32), vmem((owned, lanes), f32)),
            in_specs=[pl.BlockSpec(memory_space=pltpu.HBM)] * 15,
            out_specs=[pl.BlockSpec(memory_space=pltpu.VMEM)] * 2,
            scratch_shapes=[pltpu.SMEM(value.shape, value.dtype) for value in numbers]
            + [vmem(value.shape, value.dtype) for value in (index_row,) + streamed]
            + [
                dma((16,)),
                vmem((2, 4, slots, lanes), f32),
                vmem((2, 4, slots, lanes), f32),
                vmem((4, slots, lanes), f32),
                vmem((4, slots, lanes), f32),
                vmem((4, functions, lanes), bf16),
                vmem((4, functions, lanes), bf16),
                vmem((4, 1, lanes), f32),
                vmem((4, 1, lanes), f32),
                dma((5, 4)),
                dma((5, 4)),
                field,
                ext,
                ext,
                ext,
                ext,
                vmem((4, extent, lanes), f32),
                vmem((5 * functions, devices), bf16),
                vmem((5 * functions, lanes), jnp.int32),
                vmem((wide_count, groups, lanes), f32),
                vmem((devices, groups, lanes), f32),
                vmem((devices, 1, coarse_rows), f32),
                vmem((1, coarse_rows), f32),
                vmem((1, lanes), f32),
                vmem((devices, 1, lanes), f32),
                dma((3,)),
                dma((3,)),
                vmem((owned, faces, lanes), f32),
                vmem((owned, faces, lanes), f32),
                ext,
                field,
                pltpu.SemaphoreType.REGULAR((8,)),
            ],
            compiler_params=pltpu.CompilerParams(
                collective_id=0, has_side_effects=True, vmem_limit_bytes=65400 << 10
            ),
            name="iteration",
        )(*numbers, index_row, *streamed)
        out = jax.ShapeDtypeStruct((owned, lanes), f32)
        return pl.pallas_call(
            hand_over,
            out_shape=(out, out),
            in_specs=[pl.BlockSpec(memory_space=pltpu.VMEM)] * 2,
            out_specs=[pl.BlockSpec(memory_space=pltpu.HBM)] * 2,
            scratch_shapes=[dma((2,))],
            compiler_params=pltpu.CompilerParams(vmem_limit_bytes=1 << 20),
            name="results",
        )(*results)

    split = ("wide", "narrow")
    return jax.shard_map(
        local,
        mesh=mesh,
        in_specs=(
            P(split, None),
            P(split, None),
            P(split, None),
            P(split, None),
            P(split, None),
            P(split, None),
            P(None, split),
            P(None, split),
            P(split, None, None, None),
            P(split, None),
            P(split, None, None),
            P(split, None),
            P(split, None),
            P(split),
            P(split, None),
        ),
        out_specs=(P(split, None), P(split, None)),
        check_vma=False,
    )
```

```python
import functools

import jax
import jax.numpy as jnp
from jax import lax
from jax.experimental import pallas as pl
from jax.experimental.pallas import tpu as pltpu
from jax.sharding import PartitionSpec as P

SWEEPS = 4
MATRIX_ROWS = 4

shift_offsets = (2, 1, -1, -2)
courant = 0.9
MESH = pl.DeviceIdType.MESH
f32, bf16 = jnp.float32, jnp.bfloat16
contract_last = (((1,), (1,)), ((), ()))
plain = (((1,), (0,)), ((), ()))
PRESSURE, RESIDUAL, EXTRAS, BASIS, UPDATE = range(5)


def rounded(value):
    return value.astype(bf16).astype(f32)


def kernel(
    wide_count,
    narrow_count,
    face_hbm,
    columns_hbm,
    blocks_hbm,
    counts_hbm,
    index_hbm,
    pressure_hbm,
    right_hbm,
    conc_hbm,
    volume_hbm,
    rate_hbm,
    inject_hbm,
    trans_hbm,
    matrix_hbm,
    basis_hbm,
    inverse_hbm,
    pressure_out,
    conc_out,
    face_neighbor,
    sub_columns,
    send_blocks,
    send_counts,
    index_row,
    pressure,
    right_side,
    conc,
    volume,
    rate,
    inject,
    trans,
    matrix,
    basis,
    inverse,
    load_sem,
    outbox,
    inbox,
    extras_out,
    extras_in,
    basis_out,
    basis_in,
    update_out,
    update_in,
    margin_send,
    margin_recv,
    own,
    ext_a,
    ext_b,
    target,
    diag,
    picked,
    row_of,
    lane_of,
    partial,
    residual_in,
    value_in,
    value_mine,
    top_mine,
    top_in,
    all_send,
    all_recv,
    near_p,
    near_c,
    ext_c,
    adv,
    grow,
    near_a,
    near_b,
):
    w, n = lax.axis_index("wide"), lax.axis_index("narrow")
    devices, me = wide_count * narrow_count, w * narrow_count + n
    owned, lanes = pressure.shape
    extent = ext_a.shape[0]
    slots = outbox.shape[2]
    faces = trans.shape[0]
    functions = index_row.shape[1]
    chunks = functions // lanes
    groups = partial.shape[1]
    coarse_rows, coarse_width = inverse.shape
    coarse_lines = wide_count * groups

    def wrapped(at, count):
        return jnp.where(at >= count, at - count, at)

    def inside(offset):
        return jnp.logical_and(w + offset >= 0, w + offset < wide_count)

    def others_narrow(body):
        for step in range(1, narrow_count):
            body(w, wrapped(n + step, narrow_count))

    def signal(sem, row, column):
        pl.semaphore_signal(sem, inc=1, device_id=(row, column), device_id_type=MESH)

    barrier = pltpu.get_barrier_semaphore()

    def meet(sem, offsets):
        for offset in offsets:
            @pl.when(inside(offset))
            def _():
                signal(sem, w + offset, n)

    def met(sem, offsets, more=0):
        pl.semaphore_wait(sem, more + sum(jnp.where(inside(offset), 1, 0) for offset in offsets))

    meet(barrier, shift_offsets)
    others_narrow(lambda row, column: signal(barrier, row, column))

    loads = {}

    def load(name, source, place):
        copy = pltpu.make_async_copy(source, place, load_sem.at[len(loads)])
        copy.start()
        loads[name] = copy

    def ready(*names):
        for name in names:
            loads[name].wait()

    rest = extent - owned
    load("pressure", pressure_hbm, pressure)
    load("blocks", blocks_hbm, send_blocks)
    load("counts", counts_hbm, send_counts)
    load("columns", columns_hbm, sub_columns)
    load("index", index_hbm, index_row)
    load("matrix", matrix_hbm.at[pl.ds(0, owned)], matrix.at[pl.ds(0, owned)])
    load("right", right_hbm, right_side)
    load("conc", conc_hbm, conc)
    load("basis", basis_hbm, basis)
    load("more", matrix_hbm.at[pl.ds(owned, rest)], matrix.at[pl.ds(owned, rest)])
    load("inverse", inverse_hbm, inverse)
    load("faces", face_hbm, face_neighbor)
    load("trans", trans_hbm, trans)
    load("volume", volume_hbm, volume)
    load("rate", rate_hbm, rate)
    load("inject", inject_hbm, inject)

    boxes = (
        lambda at: (outbox.at[0, at], inbox.at[0, at]),
        lambda at: (outbox.at[1, at], inbox.at[1, at]),
        lambda at: (extras_out.at[at], extras_in.at[at]),
        lambda at: (basis_out.at[at], basis_in.at[at]),
        lambda at: (update_out.at[at], update_in.at[at]),
    )

    def margin_copy(kind, position):
        source, place = boxes[kind](position)
        return pltpu.make_async_remote_copy(
            src_ref=source,
            dst_ref=place,
            send_sem=margin_send.at[kind, position],
            recv_sem=margin_recv.at[kind, position],
            device_id=(w + shift_offsets[position], n),
            device_id_type=MESH,
        )

    slot_id = lax.broadcasted_iota(jnp.int32, (slots, lanes), 0)

    def pack(turn, rows):
        for position in range(4):
            for t in range(slots):
                outbox[turn, position, pl.ds(t, 1), :] = rows[pl.ds(send_blocks[0, position, t], 1), :]
            filled = outbox[turn, position]
            outbox[turn, position] = jnp.where(slot_id < send_counts[0, position], filled, 0.0)

    def send_margin(kind):
        for position, offset in enumerate(shift_offsets):
            @pl.when(inside(offset))
            def _():
                margin_copy(kind, position).start()

    def take_margin(kind, use, nothing):
        for position, offset in enumerate(shift_offsets):
            @pl.when(inside(-offset))
            def _():
                margin_copy(kind, position).wait_recv()
                use(position)

            @pl.when(jnp.logical_not(inside(-offset)))
            def _():
                nothing(position)

    def take_rows(turn, place):
        def use(position):
            place[pl.ds(owned + position * slots, slots), :] = inbox[turn, position]

        def nothing(position):
            place[pl.ds(owned + position * slots, slots), :] = jnp.zeros((slots, lanes), f32)

        take_margin(turn, use, nothing)

    def exchange(turn, send_from, land_in):
        def start():
            def send(row, column):
                pltpu.make_async_remote_copy(
                    src_ref=send_from(row),
                    dst_ref=land_in.at[me],
                    send_sem=all_send.at[turn],
                    recv_sem=all_recv.at[turn],
                    device_id=(row, column),
                    device_id_type=MESH,
                ).start()

            columns = [n] + [wrapped(n + step, narrow_count) for step in range(1, narrow_count)]

            @pl.loop(1, wide_count)
            def _(step):
                row = wrapped(w + step, wide_count)
                for column in columns:
                    send(row, column)

            others_narrow(send)

        others = land_in.at[pl.ds(0, devices - 1)]
        every = pltpu.make_async_remote_copy(
            src_ref=others,
            dst_ref=others,
            send_sem=all_send.at[turn],
            recv_sem=all_recv.at[turn],
            device_id=(wrapped(w + 1, wide_count), n),
            device_id_type=MESH,
        )
        return start, every.wait_recv, every.wait_send

    residuals = exchange(0, lambda row: partial.at[row], residual_in)
    values_all = exchange(1, lambda row: value_mine, value_in)
    tops = exchange(2, lambda row: top_mine, top_in)

    ready("pressure", "blocks", "counts")
    own[...] = rounded(pressure[...])
    pack(0, own)
    met(barrier, shift_offsets, narrow_count - 1)
    send_margin(PRESSURE)

    radius, rounds = 2, []
    while radius < wide_count - 1:
        rounds.append((radius, -radius))
        radius *= 2
    if rounds:
        meet(grow.at[0], rounds[0])

    ready("index")
    power = coarse_rows.bit_length() - 1

    def spread_index(part, line, place):
        tall = jnp.broadcast_to(line, (lanes, lanes)).T.astype(jnp.int32)
        rows = pl.ds(part * lanes, lanes)
        line_of = jnp.right_shift(tall, power)
        wide_id = lax.broadcasted_iota(jnp.int32, (lanes, devices), 1)
        row_of[rows, :] = jnp.where(line_of[:, :1] == wide_id, 1.0, 0.0).astype(bf16)
        lane_of[rows, :] = jnp.bitwise_and(tall, coarse_rows - 1)
        return tall

    number = index_row[...]
    number_f = number.astype(f32)
    tall_parts = [spread_index(c, number_f[:, c * lanes : (c + 1) * lanes], None) for c in range(chunks)]
    lane_id = lax.broadcasted_iota(jnp.int32, (functions, lanes), 1)
    line_hot = jnp.where(
        jnp.right_shift(number, 7) == lax.broadcasted_iota(jnp.int32, (coarse_lines, functions), 0), 1.0, 0.0
    ).astype(bf16)

    def next_round(at):
        met(grow.at[at], rounds[at])
        if at + 1 < len(rounds):
            meet(grow.at[at + 1], rounds[at + 1])

    if rounds:
        next_round(0)

    ready("conc", "basis")
    for position in range(4):
        block = send_blocks[0, position, 0]
        extras_out[position, pl.ds(0, 1), :] = conc[pl.ds(block, 1), :]
        for c in range(chunks):
            extras_out[position, pl.ds(1 + c, 1), :] = number_f[:, c * lanes : (c + 1) * lanes]
        extras_out[position, pl.ds(1 + chunks, slots - 1 - chunks), :] = jnp.zeros((slots - 1 - chunks, lanes), f32)
        basis_out[position] = basis[:, pl.ds(block * lanes, lanes)]
    send_margin(EXTRAS)
    send_margin(BASIS)

    ready("matrix")
    eye = lax.broadcasted_iota(jnp.int32, (lanes, lanes), 0) == lax.broadcasted_iota(jnp.int32, (lanes, lanes), 1)

    def diagonals(start, stop):
        @pl.loop(start, stop, unroll=4)
        def _(row):
            block = matrix[row, 0].astype(f32)
            diag[pl.ds(row, 1), :] = jnp.sum(jnp.where(eye, block, 0.0), axis=0, keepdims=True)

    diagonals(0, owned)
    for at in range(1, len(rounds)):
        next_round(at)
    last = grow.at[len(rounds)]
    others_narrow(lambda row, column: signal(last, row, column))
    ready("columns", "right")

    sub_id = lax.broadcasted_iota(jnp.int32, (8, lanes), 0)

    def dense(row, columns, vector):
        terms = [matrix[row, k].astype(f32) * vector[pl.ds(column, 1), :] for k, column in enumerate(columns)]
        total = terms[0]
        for term in terms[1:]:
            total += term
        return jnp.sum(total.T, axis=0, keepdims=True)

    def product(group, vector):
        base = pl.multiple_of(group * 8, 8)
        for i in range(MATRIX_ROWS):
            for k in range(4):
                picked[k, pl.ds(base + i, 1), :] = vector[pl.ds(sub_columns[k, base + i], 1), :]
        left = jnp.concatenate([picked[k, pl.ds(base, 8), :].astype(bf16) for k in range(4)], axis=1)
        total = jnp.zeros((8, lanes), f32)
        for i in range(0, MATRIX_ROWS, 2):
            pair = matrix[pl.ds(base + i, 2)]
            blocks = jnp.concatenate([pair[:, k].reshape(2 * lanes, lanes) for k in range(4)], axis=1)
            made = lax.dot_general(left, blocks, contract_last, preferred_element_type=f32)
            total = jnp.where(sub_id == i, made[:, :lanes], total)
            total = jnp.where(sub_id == i + 1, made[:, lanes:], total)
        for i in range(MATRIX_ROWS, 8):
            row = base + i
            total = jnp.where(sub_id == i, dense(row, [sub_columns[k, row] for k in range(4)], vector), total)
        return total

    def groups_of(count, body):
        @pl.loop(0, count // 8, unroll=4)
        def _(group):
            body(group, pl.ds(pl.multiple_of(group * 8, 8), 8))

    ext_a[pl.ds(0, owned), :] = own[...]
    take_rows(PRESSURE, ext_a)

    def residual_group(group, rows):
        own[rows, :] = rounded(right_side[rows, :] - product(group, ext_a))

    groups_of(owned, residual_group)
    pack(1, own)
    send_margin(RESIDUAL)

    flat = jnp.concatenate([own[pl.ds(b, 1), :] for b in range(owned)], axis=1)
    flat = jnp.broadcast_to(flat, (8, flat.shape[1])).astype(bf16)
    local_coarse = lax.dot_general(flat, basis[...], contract_last, preferred_element_type=f32)[0:1, :]
    tall_coarse = jnp.concatenate(
        [jnp.broadcast_to(local_coarse[:, c * lanes : (c + 1) * lanes], (lanes, lanes)).T for c in range(chunks)], axis=0
    )
    tall_index = jnp.concatenate(tall_parts, axis=0)
    placed = jnp.where(jnp.bitwise_and(tall_index, lanes - 1) == lane_id, tall_coarse, 0.0)
    high = placed.astype(bf16)
    left_over = placed - high.astype(f32)
    middle = left_over.astype(bf16)
    low = (left_over - middle.astype(f32)).astype(bf16)
    spread = lax.dot_general(
        line_hot, jnp.concatenate([high, middle, low], axis=1), plain, preferred_element_type=f32
    )
    spread = spread[:, :lanes] + spread[:, lanes : 2 * lanes] + spread[:, 2 * lanes :]
    for block in range(wide_count):
        partial[block] = spread[block * groups : (block + 1) * groups]
    pl.semaphore_wait(last, narrow_count - 1)
    residuals[0]()

    ready("more")
    diagonals(owned, extent)
    target[pl.ds(0, owned), :] = own[...]

    def use_extras(position):
        ext_c[pl.ds(owned + position * slots, slots), :] = extras_in[position]

    def no_extras(position):
        ext_c[pl.ds(owned + position * slots, slots), :] = jnp.zeros((slots, lanes), f32)
        basis_in[position] = jnp.zeros((functions, lanes), bf16)
        update_in[position] = jnp.zeros((1, lanes), f32)

    take_rows(RESIDUAL, target)
    ext_a[...] = target[...] / diag[...]
    near_a[...] = rounded(ext_a[...])

    def sweep(count, old, old_near, new, new_near):
        def body(group, rows):
            fresh = old[rows, :] + (target[rows, :] - product(group, old_near)) / diag[rows, :]
            new[rows, :] = fresh
            if new_near is not None:
                new_near[rows, :] = rounded(fresh)

        groups_of(count, body)

    sweep(extent, ext_a, near_a, ext_b, near_b)
    sweep(extent, ext_b, near_b, ext_a, near_a)

    ready("inverse")
    residual_in[me] = partial[w]
    residuals[1]()
    block_sum = jnp.sum(residual_in[...], axis=0)
    weighed = inverse[:, :lanes] * block_sum[0:1]
    for c in range(1, groups):
        weighed += inverse[:, c * lanes : (c + 1) * lanes] * block_sum[c : c + 1]
    value_mine[...] = rounded(jnp.sum(weighed.T, axis=0, keepdims=True))
    value_in[me] = value_mine[...]
    values_all[0]()

    for position in range(4):
        block = send_blocks[0, position, 0]
        row = pl.ds(block, 1)
        made = dense(block, [sub_columns[k, block] for k in range(4)], near_a)
        update_out[position] = pressure[row, :] + (ext_a[row, :] + (target[row, :] - made) / diag[row, :])
    send_margin(UPDATE)

    sweep(owned, ext_a, near_a, ext_b, None)
    own[...] = pressure[...] + ext_b[pl.ds(0, owned), :]

    ext_c[pl.ds(0, owned), :] = conc[...]
    take_margin(EXTRAS, use_extras, no_extras)
    for position in range(4):
        for c in range(chunks):
            line = ext_c[pl.ds(owned + position * slots + 1 + c, 1), :]
            spread_index((1 + position) * chunks + c, line, None)

    def gather_faces(place, field):
        @pl.loop(0, owned, unroll=4)
        def _(b):
            for f in range(faces):
                place[b, pl.ds(f, 1), :] = field[pl.ds(face_neighbor[f, b], 1), :]

    ready("faces")
    gather_faces(near_c, ext_c)
    ready("trans", "volume", "rate", "inject")
    take_margin(BASIS, lambda position: None, lambda position: None)
    target[pl.ds(owned, extent - owned), :] = jnp.zeros((extent - owned, lanes), f32)

    values_all[1]()
    coarse = value_in[...].reshape(devices, coarse_rows).astype(bf16)
    lined = lax.dot_general(row_of[...], coarse, plain, preferred_element_type=f32)
    value_lane = lax.broadcasted_iota(jnp.int32, lined.shape, 1)
    lined = jnp.where(lane_of[:, :coarse_rows] == value_lane, lined, 0.0).astype(bf16)
    chosen = lax.dot_general(
        jnp.ones((8, coarse_rows), bf16), lined, contract_last, preferred_element_type=f32
    ).astype(bf16)
    correction = lax.dot_general(chosen[:, :functions], basis[...], plain, preferred_element_type=f32)
    near = [
        lax.dot_general(
            chosen[:, (1 + position) * functions : (2 + position) * functions],
            basis_in[position],
            plain,
            preferred_element_type=f32,
        )
        for position in range(4)
    ]
    for b in range(owned):
        target[pl.ds(b, 1), :] = own[pl.ds(b, 1), :] + correction[0:1, b * lanes : (b + 1) * lanes]
    take_margin(UPDATE, lambda position: None, lambda position: None)
    for position in range(4):
        target[pl.ds(owned + position * slots, 1), :] = update_in[position] + near[position][0:1]
    pressure_out[...] = target[pl.ds(0, owned), :]
    gather_faces(near_p, target)

    @pl.loop(0, owned, unroll=4)
    def _(b):
        row = pl.ds(b, 1)
        flux = trans[:, pl.ds(pl.multiple_of(b * lanes, lanes), lanes)] * (target[row, :] - near_p[b])
        outward, inward = jnp.maximum(flux, 0.0), jnp.minimum(flux, 0.0)
        adv[row, :] = jnp.sum(outward * conc[row, :] + inward * near_c[b], axis=0, keepdims=True)
        ext_b[row, :] = jnp.sum(outward, axis=0, keepdims=True)

    cell_rate = (ext_b[pl.ds(0, owned), :] + rate[...]) / volume[...]
    top_mine[...] = jnp.max(cell_rate, axis=0, keepdims=True)
    tops[0]()
    scaled = (rate[...] * (inject[...] - conc[...]) - adv[...]) / volume[...]

    for kind in range(5):
        for position, offset in enumerate(shift_offsets):
            @pl.when(inside(offset))
            def _():
                margin_copy(kind, position).wait_send()
    residuals[2]()
    values_all[2]()
    top_in[me] = top_mine[...]
    tops[1]()
    top = jnp.max(top_in[...], axis=0)
    time_step = courant / jnp.max(top, axis=1, keepdims=True)
    conc_out[...] = conc[...] + time_step * scaled
    tops[2]()


def hand_over(pressure, conc, pressure_out, conc_out, sem):
    copies = [
        pltpu.make_async_copy(pressure, pressure_out, sem.at[0]),
        pltpu.make_async_copy(conc, conc_out, sem.at[1]),
    ]
    for copy in copies:
        copy.start()
    for copy in copies:
        copy.wait()


def solution(mesh):
    wide_count, narrow_count = mesh.shape["wide"], mesh.shape["narrow"]

    def local(
        pressure,
        right_side,
        concentration,
        pore_volume,
        well_rate,
        inject_conc,
        transmissibility,
        face_neighbor,
        sub_matrix,
        sub_columns,
        send_blocks,
        send_counts,
        basis_weights,
        coarse_index,
        coarse_inverse,
    ):
        owned, lanes = pressure.shape
        extent = sub_matrix.shape[0]
        slots = send_blocks.shape[-1]
        faces = face_neighbor.shape[0]
        functions = coarse_index.shape[0]
        coarse_rows, coarse_width = coarse_inverse.shape
        devices = wide_count * narrow_count
        groups = coarse_width // lanes
        numbers = (face_neighbor, sub_columns.T, send_blocks, send_counts)
        index_row = coarse_index.reshape(1, functions)
        streamed = (
            pressure,
            right_side,
            concentration,
            pore_volume,
            well_rate,
            inject_conc,
            transmissibility,
            sub_matrix,
            basis_weights,
            coarse_inverse,
        )
        dma, vmem = pltpu.SemaphoreType.DMA, pltpu.VMEM
        field, ext = vmem((owned, lanes), f32), vmem((extent, lanes), f32)
        results = pl.pallas_call(
            functools.partial(kernel, wide_count, narrow_count),
            out_shape=(vmem((owned, lanes), f32), vmem((owned, lanes), f32)),
            in_specs=[pl.BlockSpec(memory_space=pltpu.HBM)] * 15,
            out_specs=[pl.BlockSpec(memory_space=pltpu.VMEM)] * 2,
            scratch_shapes=[pltpu.SMEM(value.shape, value.dtype) for value in numbers]
            + [vmem(value.shape, value.dtype) for value in (index_row,) + streamed]
            + [
                dma((16,)),
                vmem((2, 4, slots, lanes), f32),
                vmem((2, 4, slots, lanes), f32),
                vmem((4, slots, lanes), f32),
                vmem((4, slots, lanes), f32),
                vmem((4, functions, lanes), bf16),
                vmem((4, functions, lanes), bf16),
                vmem((4, 1, lanes), f32),
                vmem((4, 1, lanes), f32),
                dma((5, 4)),
                dma((5, 4)),
                field,
                ext,
                ext,
                ext,
                ext,
                vmem((4, extent, lanes), f32),
                vmem((5 * functions, devices), bf16),
                vmem((5 * functions, lanes), jnp.int32),
                vmem((wide_count, groups, lanes), f32),
                vmem((devices, groups, lanes), f32),
                vmem((devices, 1, coarse_rows), f32),
                vmem((1, coarse_rows), f32),
                vmem((1, lanes), f32),
                vmem((devices, 1, lanes), f32),
                dma((3,)),
                dma((3,)),
                vmem((owned, faces, lanes), f32),
                vmem((owned, faces, lanes), f32),
                ext,
                field,
                pltpu.SemaphoreType.REGULAR((8,)),
                ext,
                ext,
            ],
            compiler_params=pltpu.CompilerParams(
                collective_id=0, has_side_effects=True, vmem_limit_bytes=65400 << 10
            ),
            name="iteration",
        )(*numbers, index_row, *streamed)
        out = jax.ShapeDtypeStruct((owned, lanes), f32)
        return pl.pallas_call(
            hand_over,
            out_shape=(out, out),
            in_specs=[pl.BlockSpec(memory_space=pltpu.VMEM)] * 2,
            out_specs=[pl.BlockSpec(memory_space=pltpu.HBM)] * 2,
            scratch_shapes=[dma((2,))],
            compiler_params=pltpu.CompilerParams(vmem_limit_bytes=1 << 20),
            name="results",
        )(*results)

    split = ("wide", "narrow")
    return jax.shard_map(
        local,
        mesh=mesh,
        in_specs=(
            P(split, None),
            P(split, None),
            P(split, None),
            P(split, None),
            P(split, None),
            P(split, None),
            P(None, split),
            P(None, split),
            P(split, None, None, None),
            P(split, None),
            P(split, None, None),
            P(split, None),
            P(split, None),
            P(split),
            P(split, None),
        ),
        out_specs=(P(split, None), P(split, None)),
        check_vma=False,
    )
```

```python
import functools

import jax
import jax.numpy as jnp
from jax import lax
from jax.experimental import pallas as pl
from jax.experimental.pallas import tpu as pltpu
from jax.sharding import PartitionSpec as P

SWEEPS = 4
MATRIX_ROWS = 4

shift_offsets = (2, 1, -1, -2)
courant = 0.9
MESH = pl.DeviceIdType.MESH
f32, bf16 = jnp.float32, jnp.bfloat16
contract_last = (((1,), (1,)), ((), ()))
plain = (((1,), (0,)), ((), ()))
PRESSURE, RESIDUAL, EXTRAS, BASIS, UPDATE = range(5)


def rounded(value):
    return value.astype(bf16).astype(f32)


def kernel(
    wide_count,
    narrow_count,
    face_hbm,
    columns_hbm,
    blocks_hbm,
    counts_hbm,
    index_hbm,
    pressure_hbm,
    right_hbm,
    conc_hbm,
    volume_hbm,
    rate_hbm,
    inject_hbm,
    trans_hbm,
    matrix_hbm,
    basis_hbm,
    inverse_hbm,
    pressure_out,
    conc_out,
    face_neighbor,
    sub_columns,
    send_blocks,
    send_counts,
    index_row,
    pressure,
    right_side,
    conc,
    volume,
    rate,
    inject,
    trans,
    matrix,
    basis,
    inverse,
    load_sem,
    outbox,
    inbox,
    extras_out,
    extras_in,
    basis_out,
    basis_in,
    update_out,
    update_in,
    margin_send,
    margin_recv,
    own,
    ext_a,
    ext_b,
    target,
    diag,
    picked,
    row_of,
    lane_of,
    partial,
    residual_in,
    value_in,
    value_mine,
    top_mine,
    top_in,
    all_send,
    all_recv,
    near_p,
    near_c,
    ext_c,
    adv,
    grow,
    near_a,
    near_b,
):
    w, n = lax.axis_index("wide"), lax.axis_index("narrow")
    devices, me = wide_count * narrow_count, w * narrow_count + n
    owned, lanes = pressure.shape
    extent = ext_a.shape[0]
    slots = outbox.shape[2]
    faces = trans.shape[0]
    functions = index_row.shape[1]
    chunks = functions // lanes
    groups = partial.shape[1]
    coarse_rows, coarse_width = inverse.shape
    coarse_lines = wide_count * groups

    def wrapped(at, count):
        return jnp.where(at >= count, at - count, at)

    def inside(offset):
        return jnp.logical_and(w + offset >= 0, w + offset < wide_count)

    def others_narrow(body):
        for step in range(1, narrow_count):
            body(w, wrapped(n + step, narrow_count))

    def signal(sem, row, column):
        pl.semaphore_signal(sem, inc=1, device_id=(row, column), device_id_type=MESH)

    barrier = pltpu.get_barrier_semaphore()

    def meet(sem, offsets):
        for offset in offsets:
            @pl.when(inside(offset))
            def _():
                signal(sem, w + offset, n)

    def met(sem, offsets, more=0):
        pl.semaphore_wait(sem, more + sum(jnp.where(inside(offset), 1, 0) for offset in offsets))

    meet(barrier, shift_offsets)
    others_narrow(lambda row, column: signal(barrier, row, column))

    loads = {}

    def load(name, source, place):
        copy = pltpu.make_async_copy(source, place, load_sem.at[len(loads)])
        copy.start()
        loads[name] = copy

    def ready(*names):
        for name in names:
            loads[name].wait()

    rest = extent - owned
    load("pressure", pressure_hbm, pressure)
    load("blocks", blocks_hbm, send_blocks)
    load("counts", counts_hbm, send_counts)
    load("columns", columns_hbm, sub_columns)
    load("index", index_hbm, index_row)
    load("matrix", matrix_hbm.at[pl.ds(0, owned)], matrix.at[pl.ds(0, owned)])
    load("right", right_hbm, right_side)
    load("conc", conc_hbm, conc)
    load("basis", basis_hbm, basis)
    load("more", matrix_hbm.at[pl.ds(owned, rest)], matrix.at[pl.ds(owned, rest)])
    load("inverse", inverse_hbm, inverse)
    load("faces", face_hbm, face_neighbor)
    load("trans", trans_hbm, trans)
    load("volume", volume_hbm, volume)
    load("rate", rate_hbm, rate)
    load("inject", inject_hbm, inject)

    boxes = (
        lambda at: (outbox.at[0, at], inbox.at[0, at]),
        lambda at: (outbox.at[1, at], inbox.at[1, at]),
        lambda at: (extras_out.at[at], extras_in.at[at]),
        lambda at: (basis_out.at[at], basis_in.at[at]),
        lambda at: (update_out.at[at], update_in.at[at]),
    )

    def margin_copy(kind, position):
        source, place = boxes[kind](position)
        return pltpu.make_async_remote_copy(
            src_ref=source,
            dst_ref=place,
            send_sem=margin_send.at[kind, position],
            recv_sem=margin_recv.at[kind, position],
            device_id=(w + shift_offsets[position], n),
            device_id_type=MESH,
        )

    slot_id = lax.broadcasted_iota(jnp.int32, (slots, lanes), 0)

    def pack(turn, rows):
        for position in range(4):
            for t in range(slots):
                outbox[turn, position, pl.ds(t, 1), :] = rows[pl.ds(send_blocks[0, position, t], 1), :]
            filled = outbox[turn, position]
            outbox[turn, position] = jnp.where(slot_id < send_counts[0, position], filled, 0.0)

    def send_margin(kind):
        for position, offset in enumerate(shift_offsets):
            @pl.when(inside(offset))
            def _():
                margin_copy(kind, position).start()

    def take_margin(kind, use, nothing):
        for position, offset in enumerate(shift_offsets):
            @pl.when(inside(-offset))
            def _():
                margin_copy(kind, position).wait_recv()
                use(position)

            @pl.when(jnp.logical_not(inside(-offset)))
            def _():
                nothing(position)

    def take_rows(turn, place):
        def use(position):
            place[pl.ds(owned + position * slots, slots), :] = inbox[turn, position]

        def nothing(position):
            place[pl.ds(owned + position * slots, slots), :] = jnp.zeros((slots, lanes), f32)

        take_margin(turn, use, nothing)

    def exchange(turn, send_from, land_in):
        def start():
            def send(row, column):
                pltpu.make_async_remote_copy(
                    src_ref=send_from(row),
                    dst_ref=land_in.at[me],
                    send_sem=all_send.at[turn],
                    recv_sem=all_recv.at[turn],
                    device_id=(row, column),
                    device_id_type=MESH,
                ).start()

            columns = [n] + [wrapped(n + step, narrow_count) for step in range(1, narrow_count)]

            @pl.loop(1, wide_count)
            def _(step):
                row = wrapped(w + step, wide_count)
                for column in columns:
                    send(row, column)

            others_narrow(send)

        others = land_in.at[pl.ds(0, devices - 1)]
        every = pltpu.make_async_remote_copy(
            src_ref=others,
            dst_ref=others,
            send_sem=all_send.at[turn],
            recv_sem=all_recv.at[turn],
            device_id=(wrapped(w + 1, wide_count), n),
            device_id_type=MESH,
        )
        return start, every.wait_recv, every.wait_send

    residuals = exchange(0, lambda row: partial.at[row], residual_in)
    values_all = exchange(1, lambda row: value_mine, value_in)
    tops = exchange(2, lambda row: top_mine, top_in)

    ready("pressure", "blocks", "counts")
    own[...] = rounded(pressure[...])
    pack(0, own)
    met(barrier, shift_offsets, narrow_count - 1)
    send_margin(PRESSURE)

    radius, rounds = 2, []
    while radius < wide_count - 1:
        rounds.append((radius, -radius))
        radius *= 2
    if rounds:
        meet(grow.at[0], rounds[0])

    ready("index")
    power = coarse_rows.bit_length() - 1

    def spread_index(part, line, place):
        tall = jnp.broadcast_to(line, (lanes, lanes)).T.astype(jnp.int32)
        rows = pl.ds(part * lanes, lanes)
        line_of = jnp.right_shift(tall, power)
        wide_id = lax.broadcasted_iota(jnp.int32, (lanes, devices), 1)
        row_of[rows, :] = jnp.where(line_of[:, :1] == wide_id, 1.0, 0.0).astype(bf16)
        lane_of[rows, :] = jnp.bitwise_and(tall, coarse_rows - 1)
        return tall

    number = index_row[...]
    number_f = number.astype(f32)
    tall_parts = [spread_index(c, number_f[:, c * lanes : (c + 1) * lanes], None) for c in range(chunks)]
    lane_id = lax.broadcasted_iota(jnp.int32, (functions, lanes), 1)
    line_hot = jnp.where(
        jnp.right_shift(number, 7) == lax.broadcasted_iota(jnp.int32, (coarse_lines, functions), 0), 1.0, 0.0
    ).astype(bf16)

    def next_round(at):
        met(grow.at[at], rounds[at])
        if at + 1 < len(rounds):
            meet(grow.at[at + 1], rounds[at + 1])

    if rounds:
        next_round(0)

    ready("conc", "basis")
    for position in range(4):
        block = send_blocks[0, position, 0]
        extras_out[position, pl.ds(0, 1), :] = conc[pl.ds(block, 1), :]
        for c in range(chunks):
            extras_out[position, pl.ds(1 + c, 1), :] = number_f[:, c * lanes : (c + 1) * lanes]
        extras_out[position, pl.ds(1 + chunks, slots - 1 - chunks), :] = jnp.zeros((slots - 1 - chunks, lanes), f32)
        basis_out[position] = basis[:, pl.ds(block * lanes, lanes)]
    send_margin(EXTRAS)
    send_margin(BASIS)

    ready("matrix")
    eye = lax.broadcasted_iota(jnp.int32, (lanes, lanes), 0) == lax.broadcasted_iota(jnp.int32, (lanes, lanes), 1)

    def diagonals(start, stop):
        @pl.loop(start, stop, unroll=4)
        def _(row):
            block = matrix[row, 0].astype(f32)
            diag[pl.ds(row, 1), :] = jnp.sum(jnp.where(eye, block, 0.0), axis=0, keepdims=True)

    diagonals(0, owned)
    for at in range(1, len(rounds)):
        next_round(at)
    last = grow.at[len(rounds)]
    others_narrow(lambda row, column: signal(last, row, column))
    ready("columns", "right")

    sub_id = lax.broadcasted_iota(jnp.int32, (8, lanes), 0)

    def dense(row, columns, vector):
        terms = [matrix[row, k].astype(f32) * vector[pl.ds(column, 1), :] for k, column in enumerate(columns)]
        total = terms[0]
        for term in terms[1:]:
            total += term
        return jnp.sum(total.T, axis=0, keepdims=True)

    def product(group, vector):
        base = pl.multiple_of(group * 8, 8)
        for i in range(MATRIX_ROWS):
            for k in range(4):
                picked[k, pl.ds(base + i, 1), :] = vector[pl.ds(sub_columns[k, base + i], 1), :]
        left = jnp.concatenate([picked[k, pl.ds(base, 8), :].astype(bf16) for k in range(4)], axis=1)
        total = jnp.zeros((8, lanes), f32)
        for i in range(0, MATRIX_ROWS, 2):
            pair = matrix[pl.ds(base + i, 2)]
            blocks = jnp.concatenate([pair[:, k].reshape(2 * lanes, lanes) for k in range(4)], axis=1)
            made = lax.dot_general(left, blocks, contract_last, preferred_element_type=f32)
            total = jnp.where(sub_id == i, made[:, :lanes], total)
            total = jnp.where(sub_id == i + 1, made[:, lanes:], total)
        for i in range(MATRIX_ROWS, 8):
            row = base + i
            total = jnp.where(sub_id == i, dense(row, [sub_columns[k, row] for k in range(4)], vector), total)
        return total

    def groups_of(count, body, unroll=4):
        @pl.loop(0, count // 8, unroll=unroll)
        def _(group):
            body(group, pl.ds(pl.multiple_of(group * 8, 8), 8))

    ext_a[pl.ds(0, owned), :] = own[...]
    take_rows(PRESSURE, ext_a)

    def residual_group(group, rows):
        own[rows, :] = rounded(right_side[rows, :] - product(group, ext_a))

    groups_of(owned, residual_group, 2)
    pack(1, own)
    send_margin(RESIDUAL)

    flat = jnp.concatenate([own[pl.ds(b, 1), :] for b in range(owned)], axis=1)
    flat = jnp.broadcast_to(flat, (8, flat.shape[1])).astype(bf16)
    local_coarse = lax.dot_general(flat, basis[...], contract_last, preferred_element_type=f32)[0:1, :]
    tall_coarse = jnp.concatenate(
        [jnp.broadcast_to(local_coarse[:, c * lanes : (c + 1) * lanes], (lanes, lanes)).T for c in range(chunks)], axis=0
    )
    tall_index = jnp.concatenate(tall_parts, axis=0)
    placed = jnp.where(jnp.bitwise_and(tall_index, lanes - 1) == lane_id, tall_coarse, 0.0)
    high = placed.astype(bf16)
    left_over = placed - high.astype(f32)
    middle = left_over.astype(bf16)
    low = (left_over - middle.astype(f32)).astype(bf16)
    spread = lax.dot_general(
        line_hot, jnp.concatenate([high, middle, low], axis=1), plain, preferred_element_type=f32
    )
    spread = spread[:, :lanes] + spread[:, lanes : 2 * lanes] + spread[:, 2 * lanes :]
    for block in range(wide_count):
        partial[block] = spread[block * groups : (block + 1) * groups]
    pl.semaphore_wait(last, narrow_count - 1)
    residuals[0]()

    ready("more")
    diagonals(owned, extent)
    target[pl.ds(0, owned), :] = own[...]

    def use_extras(position):
        ext_c[pl.ds(owned + position * slots, slots), :] = extras_in[position]

    def no_extras(position):
        ext_c[pl.ds(owned + position * slots, slots), :] = jnp.zeros((slots, lanes), f32)
        basis_in[position] = jnp.zeros((functions, lanes), bf16)
        update_in[position] = jnp.zeros((1, lanes), f32)

    take_rows(RESIDUAL, target)
    ext_a[...] = target[...] / diag[...]
    near_a[...] = rounded(ext_a[...])

    def sweep(count, old, old_near, new, new_near):
        def body(group, rows):
            fresh = old[rows, :] + (target[rows, :] - product(group, old_near)) / diag[rows, :]
            new[rows, :] = fresh
            if new_near is not None:
                new_near[rows, :] = rounded(fresh)

        groups_of(count, body, 4 if new_near is not None else 2)

    sweep(extent, ext_a, near_a, ext_b, near_b)
    sweep(extent, ext_b, near_b, ext_a, near_a)

    ready("inverse")
    residual_in[me] = partial[w]
    residuals[1]()
    block_sum = jnp.sum(residual_in[...], axis=0)
    weighed = inverse[:, :lanes] * block_sum[0:1]
    for c in range(1, groups):
        weighed += inverse[:, c * lanes : (c + 1) * lanes] * block_sum[c : c + 1]
    value_mine[...] = rounded(jnp.sum(weighed.T, axis=0, keepdims=True))
    value_in[me] = value_mine[...]
    values_all[0]()

    for position in range(4):
        block = send_blocks[0, position, 0]
        row = pl.ds(block, 1)
        made = dense(block, [sub_columns[k, block] for k in range(4)], near_a)
        update_out[position] = pressure[row, :] + (ext_a[row, :] + (target[row, :] - made) / diag[row, :])
    send_margin(UPDATE)

    sweep(owned, ext_a, near_a, ext_b, None)
    own[...] = pressure[...] + ext_b[pl.ds(0, owned), :]

    ext_c[pl.ds(0, owned), :] = conc[...]
    take_margin(EXTRAS, use_extras, no_extras)
    for position in range(4):
        for c in range(chunks):
            line = ext_c[pl.ds(owned + position * slots + 1 + c, 1), :]
            spread_index((1 + position) * chunks + c, line, None)

    def gather_faces(place, field):
        @pl.loop(0, owned, unroll=4)
        def _(b):
            for f in range(faces):
                place[b, pl.ds(f, 1), :] = field[pl.ds(face_neighbor[f, b], 1), :]

    ready("faces")
    gather_faces(near_c, ext_c)
    ready("trans", "volume", "rate", "inject")
    take_margin(BASIS, lambda position: None, lambda position: None)
    target[pl.ds(owned, extent - owned), :] = jnp.zeros((extent - owned, lanes), f32)

    values_all[1]()
    coarse = value_in[...].reshape(devices, coarse_rows).astype(bf16)
    lined = lax.dot_general(row_of[...], coarse, plain, preferred_element_type=f32)
    value_lane = lax.broadcasted_iota(jnp.int32, lined.shape, 1)
    lined = jnp.where(lane_of[:, :coarse_rows] == value_lane, lined, 0.0).astype(bf16)
    chosen = lax.dot_general(
        jnp.ones((8, coarse_rows), bf16), lined, contract_last, preferred_element_type=f32
    ).astype(bf16)
    correction = lax.dot_general(chosen[:, :functions], basis[...], plain, preferred_element_type=f32)
    near = [
        lax.dot_general(
            chosen[:, (1 + position) * functions : (2 + position) * functions],
            basis_in[position],
            plain,
            preferred_element_type=f32,
        )
        for position in range(4)
    ]
    for b in range(owned):
        target[pl.ds(b, 1), :] = own[pl.ds(b, 1), :] + correction[0:1, b * lanes : (b + 1) * lanes]
    take_margin(UPDATE, lambda position: None, lambda position: None)
    for position in range(4):
        target[pl.ds(owned + position * slots, 1), :] = update_in[position] + near[position][0:1]
    pressure_out[...] = target[pl.ds(0, owned), :]
    gather_faces(near_p, target)

    @pl.loop(0, owned, unroll=4)
    def _(b):
        row = pl.ds(b, 1)
        flux = trans[:, pl.ds(pl.multiple_of(b * lanes, lanes), lanes)] * (target[row, :] - near_p[b])
        outward, inward = jnp.maximum(flux, 0.0), jnp.minimum(flux, 0.0)
        adv[row, :] = jnp.sum(outward * conc[row, :] + inward * near_c[b], axis=0, keepdims=True)
        ext_b[row, :] = jnp.sum(outward, axis=0, keepdims=True)

    cell_rate = (ext_b[pl.ds(0, owned), :] + rate[...]) / volume[...]
    top_mine[...] = jnp.max(cell_rate, axis=0, keepdims=True)
    tops[0]()
    scaled = (rate[...] * (inject[...] - conc[...]) - adv[...]) / volume[...]

    for kind in range(5):
        for position, offset in enumerate(shift_offsets):
            @pl.when(inside(offset))
            def _():
                margin_copy(kind, position).wait_send()
    residuals[2]()
    values_all[2]()
    top_in[me] = top_mine[...]
    tops[1]()
    top = jnp.max(top_in[...], axis=0)
    time_step = courant / jnp.max(top, axis=1, keepdims=True)
    conc_out[...] = conc[...] + time_step * scaled
    tops[2]()


def hand_over(pressure, conc, pressure_out, conc_out, sem):
    copies = [
        pltpu.make_async_copy(pressure, pressure_out, sem.at[0]),
        pltpu.make_async_copy(conc, conc_out, sem.at[1]),
    ]
    for copy in copies:
        copy.start()
    for copy in copies:
        copy.wait()


def solution(mesh):
    wide_count, narrow_count = mesh.shape["wide"], mesh.shape["narrow"]

    def local(
        pressure,
        right_side,
        concentration,
        pore_volume,
        well_rate,
        inject_conc,
        transmissibility,
        face_neighbor,
        sub_matrix,
        sub_columns,
        send_blocks,
        send_counts,
        basis_weights,
        coarse_index,
        coarse_inverse,
    ):
        owned, lanes = pressure.shape
        extent = sub_matrix.shape[0]
        slots = send_blocks.shape[-1]
        faces = face_neighbor.shape[0]
        functions = coarse_index.shape[0]
        coarse_rows, coarse_width = coarse_inverse.shape
        devices = wide_count * narrow_count
        groups = coarse_width // lanes
        numbers = (face_neighbor, sub_columns.T, send_blocks, send_counts)
        index_row = coarse_index.reshape(1, functions)
        streamed = (
            pressure,
            right_side,
            concentration,
            pore_volume,
            well_rate,
            inject_conc,
            transmissibility,
            sub_matrix,
            basis_weights,
            coarse_inverse,
        )
        dma, vmem = pltpu.SemaphoreType.DMA, pltpu.VMEM
        field, ext = vmem((owned, lanes), f32), vmem((extent, lanes), f32)
        results = pl.pallas_call(
            functools.partial(kernel, wide_count, narrow_count),
            out_shape=(vmem((owned, lanes), f32), vmem((owned, lanes), f32)),
            in_specs=[pl.BlockSpec(memory_space=pltpu.HBM)] * 15,
            out_specs=[pl.BlockSpec(memory_space=pltpu.VMEM)] * 2,
            scratch_shapes=[pltpu.SMEM(value.shape, value.dtype) for value in numbers]
            + [vmem(value.shape, value.dtype) for value in (index_row,) + streamed]
            + [
                dma((16,)),
                vmem((2, 4, slots, lanes), f32),
                vmem((2, 4, slots, lanes), f32),
                vmem((4, slots, lanes), f32),
                vmem((4, slots, lanes), f32),
                vmem((4, functions, lanes), bf16),
                vmem((4, functions, lanes), bf16),
                vmem((4, 1, lanes), f32),
                vmem((4, 1, lanes), f32),
                dma((5, 4)),
                dma((5, 4)),
                field,
                ext,
                ext,
                ext,
                ext,
                vmem((4, extent, lanes), f32),
                vmem((5 * functions, devices), bf16),
                vmem((5 * functions, lanes), jnp.int32),
                vmem((wide_count, groups, lanes), f32),
                vmem((devices, groups, lanes), f32),
                vmem((devices, 1, coarse_rows), f32),
                vmem((1, coarse_rows), f32),
                vmem((1, lanes), f32),
                vmem((devices, 1, lanes), f32),
                dma((3,)),
                dma((3,)),
                vmem((owned, faces, lanes), f32),
                vmem((owned, faces, lanes), f32),
                ext,
                field,
                pltpu.SemaphoreType.REGULAR((8,)),
                ext,
                ext,
            ],
            compiler_params=pltpu.CompilerParams(
                collective_id=0, has_side_effects=True, vmem_limit_bytes=65400 << 10
            ),
            name="iteration",
        )(*numbers, index_row, *streamed)
        out = jax.ShapeDtypeStruct((owned, lanes), f32)
        return pl.pallas_call(
            hand_over,
            out_shape=(out, out),
            in_specs=[pl.BlockSpec(memory_space=pltpu.VMEM)] * 2,
            out_specs=[pl.BlockSpec(memory_space=pltpu.HBM)] * 2,
            scratch_shapes=[dma((2,))],
            compiler_params=pltpu.CompilerParams(vmem_limit_bytes=1 << 20),
            name="results",
        )(*results)

    split = ("wide", "narrow")
    return jax.shard_map(
        local,
        mesh=mesh,
        in_specs=(
            P(split, None),
            P(split, None),
            P(split, None),
            P(split, None),
            P(split, None),
            P(split, None),
            P(None, split),
            P(None, split),
            P(split, None, None, None),
            P(split, None),
            P(split, None, None),
            P(split, None),
            P(split, None),
            P(split),
            P(split, None),
        ),
        out_specs=(P(split, None), P(split, None)),
        check_vma=False,
    )
```

```python
import functools

import jax
import jax.numpy as jnp
from jax import lax
from jax.experimental import pallas as pl
from jax.experimental.pallas import tpu as pltpu
from jax.sharding import PartitionSpec as P

SWEEPS = 4
MATRIX_ROWS = 4

shift_offsets = (2, 1, -1, -2)
courant = 0.9
MESH = pl.DeviceIdType.MESH
f32, bf16 = jnp.float32, jnp.bfloat16
contract_last = (((1,), (1,)), ((), ()))
plain = (((1,), (0,)), ((), ()))
PRESSURE, RESIDUAL, EXTRAS, BASIS, UPDATE = range(5)


def rounded(value):
    return value.astype(bf16).astype(f32)


def kernel(
    wide_count,
    narrow_count,
    face_hbm,
    columns_hbm,
    blocks_hbm,
    counts_hbm,
    index_hbm,
    pressure_hbm,
    right_hbm,
    conc_hbm,
    volume_hbm,
    rate_hbm,
    inject_hbm,
    trans_hbm,
    matrix_hbm,
    basis_hbm,
    inverse_hbm,
    pressure_out,
    conc_out,
    face_neighbor,
    sub_columns,
    send_blocks,
    send_counts,
    index_row,
    pressure,
    right_side,
    conc,
    volume,
    rate,
    inject,
    trans,
    matrix,
    basis,
    inverse,
    load_sem,
    outbox,
    inbox,
    extras_out,
    extras_in,
    basis_out,
    basis_in,
    update_out,
    update_in,
    margin_send,
    margin_recv,
    own,
    ext_a,
    ext_b,
    target,
    diag,
    picked,
    row_of,
    lane_of,
    partial,
    residual_in,
    value_in,
    value_mine,
    top_mine,
    top_in,
    all_send,
    all_recv,
    near_p,
    near_c,
    ext_c,
    adv,
    grow,
    near_a,
    near_b,
):
    w, n = lax.axis_index("wide"), lax.axis_index("narrow")
    devices, me = wide_count * narrow_count, w * narrow_count + n
    owned, lanes = pressure.shape
    extent = ext_a.shape[0]
    slots = outbox.shape[2]
    faces = trans.shape[0]
    functions = index_row.shape[1]
    chunks = functions // lanes
    groups = partial.shape[1]
    coarse_rows, coarse_width = inverse.shape
    coarse_lines = wide_count * groups

    def wrapped(at, count):
        return jnp.where(at >= count, at - count, at)

    def inside(offset):
        return jnp.logical_and(w + offset >= 0, w + offset < wide_count)

    def others_narrow(body):
        for step in range(1, narrow_count):
            body(w, wrapped(n + step, narrow_count))

    def signal(sem, row, column):
        pl.semaphore_signal(sem, inc=1, device_id=(row, column), device_id_type=MESH)

    barrier = pltpu.get_barrier_semaphore()

    def meet(sem, offsets):
        for offset in offsets:
            @pl.when(inside(offset))
            def _():
                signal(sem, w + offset, n)

    def met(sem, offsets, more=0):
        pl.semaphore_wait(sem, more + sum(jnp.where(inside(offset), 1, 0) for offset in offsets))

    meet(barrier, shift_offsets)
    others_narrow(lambda row, column: signal(barrier, row, column))

    loads = {}

    def load(name, source, place):
        copy = pltpu.make_async_copy(source, place, load_sem.at[len(loads)])
        copy.start()
        loads[name] = copy

    def ready(*names):
        for name in names:
            loads[name].wait()

    rest = extent - owned
    load("pressure", pressure_hbm, pressure)
    load("blocks", blocks_hbm, send_blocks)
    load("counts", counts_hbm, send_counts)
    load("columns", columns_hbm, sub_columns)
    load("index", index_hbm, index_row)
    load("matrix", matrix_hbm.at[pl.ds(0, owned)], matrix.at[pl.ds(0, owned)])
    load("right", right_hbm, right_side)
    load("conc", conc_hbm, conc)
    load("basis", basis_hbm, basis)
    load("more", matrix_hbm.at[pl.ds(owned, rest)], matrix.at[pl.ds(owned, rest)])
    load("inverse", inverse_hbm, inverse)
    load("faces", face_hbm, face_neighbor)
    load("trans", trans_hbm, trans)
    load("volume", volume_hbm, volume)
    load("rate", rate_hbm, rate)
    load("inject", inject_hbm, inject)

    boxes = (
        lambda at: (outbox.at[0, at], inbox.at[0, at]),
        lambda at: (outbox.at[1, at], inbox.at[1, at]),
        lambda at: (extras_out.at[at], extras_in.at[at]),
        lambda at: (basis_out.at[at], basis_in.at[at]),
        lambda at: (update_out.at[at], update_in.at[at]),
    )

    def margin_copy(kind, position):
        source, place = boxes[kind](position)
        return pltpu.make_async_remote_copy(
            src_ref=source,
            dst_ref=place,
            send_sem=margin_send.at[kind, position],
            recv_sem=margin_recv.at[kind, position],
            device_id=(w + shift_offsets[position], n),
            device_id_type=MESH,
        )

    slot_id = lax.broadcasted_iota(jnp.int32, (slots, lanes), 0)

    def pack(turn, rows):
        for position in range(4):
            for t in range(slots):
                outbox[turn, position, pl.ds(t, 1), :] = rows[pl.ds(send_blocks[0, position, t], 1), :]
            filled = outbox[turn, position]
            outbox[turn, position] = jnp.where(slot_id < send_counts[0, position], filled, 0.0)

    def send_margin(kind):
        for position, offset in enumerate(shift_offsets):
            @pl.when(inside(offset))
            def _():
                margin_copy(kind, position).start()

    def take_margin(kind, use, nothing):
        for position, offset in enumerate(shift_offsets):
            @pl.when(inside(-offset))
            def _():
                margin_copy(kind, position).wait_recv()
                use(position)

            @pl.when(jnp.logical_not(inside(-offset)))
            def _():
                nothing(position)

    def take_rows(turn, place):
        def use(position):
            place[pl.ds(owned + position * slots, slots), :] = inbox[turn, position]

        def nothing(position):
            place[pl.ds(owned + position * slots, slots), :] = jnp.zeros((slots, lanes), f32)

        take_margin(turn, use, nothing)

    def exchange(turn, send_from, land_in):
        def start():
            def send(row, column):
                pltpu.make_async_remote_copy(
                    src_ref=send_from(row),
                    dst_ref=land_in.at[me],
                    send_sem=all_send.at[turn],
                    recv_sem=all_recv.at[turn],
                    device_id=(row, column),
                    device_id_type=MESH,
                ).start()

            columns = [n] + [wrapped(n + step, narrow_count) for step in range(1, narrow_count)]

            @pl.loop(1, wide_count, unroll=wide_count - 1 if wide_count <= 8 else 1)
            def _(step):
                row = wrapped(w + step, wide_count)
                for column in columns:
                    send(row, column)

            others_narrow(send)

        others = land_in.at[pl.ds(0, devices - 1)]
        every = pltpu.make_async_remote_copy(
            src_ref=others,
            dst_ref=others,
            send_sem=all_send.at[turn],
            recv_sem=all_recv.at[turn],
            device_id=(wrapped(w + 1, wide_count), n),
            device_id_type=MESH,
        )
        return start, every.wait_recv, every.wait_send

    residuals = exchange(0, lambda row: partial.at[row], residual_in)
    values_all = exchange(1, lambda row: value_mine, value_in)
    tops = exchange(2, lambda row: top_mine, top_in)

    ready("pressure", "blocks", "counts")
    own[...] = rounded(pressure[...])
    pack(0, own)
    met(barrier, shift_offsets, narrow_count - 1)
    send_margin(PRESSURE)

    radius, rounds = 2, []
    while radius < wide_count - 1:
        rounds.append((radius, -radius))
        radius *= 2
    if rounds:
        meet(grow.at[0], rounds[0])

    ready("index")
    power = coarse_rows.bit_length() - 1

    def spread_index(part, line, place):
        tall = jnp.broadcast_to(line, (lanes, lanes)).T.astype(jnp.int32)
        rows = pl.ds(part * lanes, lanes)
        line_of = jnp.right_shift(tall, power)
        wide_id = lax.broadcasted_iota(jnp.int32, (lanes, devices), 1)
        row_of[rows, :] = jnp.where(line_of[:, :1] == wide_id, 1.0, 0.0).astype(bf16)
        lane_of[rows, :] = jnp.bitwise_and(tall, coarse_rows - 1)
        return tall

    number = index_row[...]
    number_f = number.astype(f32)
    tall_parts = [spread_index(c, number_f[:, c * lanes : (c + 1) * lanes], None) for c in range(chunks)]
    lane_id = lax.broadcasted_iota(jnp.int32, (functions, lanes), 1)
    line_hot = jnp.where(
        jnp.right_shift(number, 7) == lax.broadcasted_iota(jnp.int32, (coarse_lines, functions), 0), 1.0, 0.0
    ).astype(bf16)

    def next_round(at):
        met(grow.at[at], rounds[at])
        if at + 1 < len(rounds):
            meet(grow.at[at + 1], rounds[at + 1])

    if rounds:
        next_round(0)

    ready("conc", "basis")
    for position in range(4):
        block = send_blocks[0, position, 0]
        extras_out[position, pl.ds(0, 1), :] = conc[pl.ds(block, 1), :]
        for c in range(chunks):
            extras_out[position, pl.ds(1 + c, 1), :] = number_f[:, c * lanes : (c + 1) * lanes]
        extras_out[position, pl.ds(1 + chunks, slots - 1 - chunks), :] = jnp.zeros((slots - 1 - chunks, lanes), f32)
        basis_out[position] = basis[:, pl.ds(block * lanes, lanes)]
    send_margin(EXTRAS)
    send_margin(BASIS)

    ready("matrix")
    eye = lax.broadcasted_iota(jnp.int32, (lanes, lanes), 0) == lax.broadcasted_iota(jnp.int32, (lanes, lanes), 1)

    def diagonals(start, stop):
        @pl.loop(start, stop, unroll=4)
        def _(row):
            block = matrix[row, 0].astype(f32)
            diag[pl.ds(row, 1), :] = jnp.sum(jnp.where(eye, block, 0.0), axis=0, keepdims=True)

    diagonals(0, owned)
    for at in range(1, len(rounds)):
        next_round(at)
    last = grow.at[len(rounds)]
    others_narrow(lambda row, column: signal(last, row, column))
    ready("columns", "right")

    sub_id = lax.broadcasted_iota(jnp.int32, (8, lanes), 0)

    def dense(row, columns, vector):
        terms = [matrix[row, k].astype(f32) * vector[pl.ds(column, 1), :] for k, column in enumerate(columns)]
        total = terms[0]
        for term in terms[1:]:
            total += term
        return jnp.sum(total.T, axis=0, keepdims=True)

    def product(group, vector):
        base = pl.multiple_of(group * 8, 8)
        for i in range(MATRIX_ROWS):
            for k in range(4):
                picked[k, pl.ds(base + i, 1), :] = vector[pl.ds(sub_columns[k, base + i], 1), :]
        left = jnp.concatenate([picked[k, pl.ds(base, 8), :].astype(bf16) for k in range(4)], axis=1)
        total = jnp.zeros((8, lanes), f32)
        for i in range(0, MATRIX_ROWS, 2):
            pair = matrix[pl.ds(base + i, 2)]
            blocks = jnp.concatenate([pair[:, k].reshape(2 * lanes, lanes) for k in range(4)], axis=1)
            made = lax.dot_general(left, blocks, contract_last, preferred_element_type=f32)
            total = jnp.where(sub_id == i, made[:, :lanes], total)
            total = jnp.where(sub_id == i + 1, made[:, lanes:], total)
        for i in range(MATRIX_ROWS, 8):
            row = base + i
            total = jnp.where(sub_id == i, dense(row, [sub_columns[k, row] for k in range(4)], vector), total)
        return total

    def groups_of(count, body, unroll=4):
        @pl.loop(0, count // 8, unroll=unroll)
        def _(group):
            body(group, pl.ds(pl.multiple_of(group * 8, 8), 8))

    ext_a[pl.ds(0, owned), :] = own[...]
    take_rows(PRESSURE, ext_a)

    def residual_group(group, rows):
        own[rows, :] = rounded(right_side[rows, :] - product(group, ext_a))

    groups_of(owned, residual_group, 2)
    pack(1, own)
    send_margin(RESIDUAL)

    dense_from = owned - owned // 2
    flat = jnp.concatenate([own[pl.ds(b, 1), :] for b in range(dense_from)], axis=1)
    flat = jnp.broadcast_to(flat, (8, flat.shape[1])).astype(bf16)
    tall_part = jnp.zeros((functions, lanes), f32)
    for b in range(dense_from, owned):
        tall_part += basis[:, b * lanes : (b + 1) * lanes].astype(f32) * own[pl.ds(b, 1), :]
    local_coarse = lax.dot_general(flat, basis[:, : dense_from * lanes], contract_last, preferred_element_type=f32)[0:1, :]
    tall_coarse = jnp.concatenate(
        [jnp.broadcast_to(local_coarse[:, c * lanes : (c + 1) * lanes], (lanes, lanes)).T for c in range(chunks)], axis=0
    )
    tall_coarse += jnp.sum(tall_part, axis=1, keepdims=True)
    tall_index = jnp.concatenate(tall_parts, axis=0)
    placed = jnp.where(jnp.bitwise_and(tall_index, lanes - 1) == lane_id, tall_coarse, 0.0)
    high = placed.astype(bf16)
    left_over = placed - high.astype(f32)
    middle = left_over.astype(bf16)
    low = (left_over - middle.astype(f32)).astype(bf16)
    spread = lax.dot_general(
        line_hot, jnp.concatenate([high, middle, low], axis=1), plain, preferred_element_type=f32
    )
    spread = spread[:, :lanes] + spread[:, lanes : 2 * lanes] + spread[:, 2 * lanes :]
    for block in range(wide_count):
        partial[block] = spread[block * groups : (block + 1) * groups]
    pl.semaphore_wait(last, narrow_count - 1)
    residuals[0]()

    ready("more")
    diagonals(owned, extent)
    target[pl.ds(0, owned), :] = own[...]

    def use_extras(position):
        ext_c[pl.ds(owned + position * slots, slots), :] = extras_in[position]

    def no_extras(position):
        ext_c[pl.ds(owned + position * slots, slots), :] = jnp.zeros((slots, lanes), f32)
        basis_in[position] = jnp.zeros((functions, lanes), bf16)
        update_in[position] = jnp.zeros((1, lanes), f32)

    take_rows(RESIDUAL, target)
    ext_a[...] = target[...] / diag[...]
    near_a[...] = rounded(ext_a[...])

    def sweep(count, old, old_near, new, new_near):
        def body(group, rows):
            fresh = old[rows, :] + (target[rows, :] - product(group, old_near)) / diag[rows, :]
            new[rows, :] = fresh
            if new_near is not None:
                new_near[rows, :] = rounded(fresh)

        groups_of(count, body, 4 if new_near is not None else 2)

    sweep(extent, ext_a, near_a, ext_b, near_b)
    sweep(extent, ext_b, near_b, ext_a, near_a)

    ready("inverse")
    residual_in[me] = partial[w]
    residuals[1]()
    block_sum = jnp.sum(residual_in[...], axis=0)
    weighed = inverse[:, :lanes] * block_sum[0:1]
    for c in range(1, groups):
        weighed += inverse[:, c * lanes : (c + 1) * lanes] * block_sum[c : c + 1]
    value_mine[...] = rounded(jnp.sum(weighed.T, axis=0, keepdims=True))
    value_in[me] = value_mine[...]
    values_all[0]()

    for position in range(4):
        block = send_blocks[0, position, 0]
        row = pl.ds(block, 1)
        made = dense(block, [sub_columns[k, block] for k in range(4)], near_a)
        update_out[position] = pressure[row, :] + (ext_a[row, :] + (target[row, :] - made) / diag[row, :])
    send_margin(UPDATE)

    sweep(owned, ext_a, near_a, ext_b, None)
    own[...] = pressure[...] + ext_b[pl.ds(0, owned), :]

    ext_c[pl.ds(0, owned), :] = conc[...]
    take_margin(EXTRAS, use_extras, no_extras)
    for position in range(4):
        for c in range(chunks):
            line = ext_c[pl.ds(owned + position * slots + 1 + c, 1), :]
            spread_index((1 + position) * chunks + c, line, None)

    def gather_faces(place, field):
        @pl.loop(0, owned, unroll=4)
        def _(b):
            for f in range(faces):
                place[b, pl.ds(f, 1), :] = field[pl.ds(face_neighbor[f, b], 1), :]

    ready("faces")
    gather_faces(near_c, ext_c)
    ready("trans", "volume", "rate", "inject")
    take_margin(BASIS, lambda position: None, lambda position: None)
    target[pl.ds(owned, extent - owned), :] = jnp.zeros((extent - owned, lanes), f32)

    values_all[1]()
    coarse = value_in[...].reshape(devices, coarse_rows).astype(bf16)
    lined = lax.dot_general(row_of[...], coarse, plain, preferred_element_type=f32)
    value_lane = lax.broadcasted_iota(jnp.int32, lined.shape, 1)
    lined = jnp.where(lane_of[:, :coarse_rows] == value_lane, lined, 0.0).astype(bf16)
    chosen = lax.dot_general(
        jnp.ones((8, coarse_rows), bf16), lined, contract_last, preferred_element_type=f32
    ).astype(bf16)
    correction = lax.dot_general(chosen[:, :functions], basis[...], plain, preferred_element_type=f32)
    near = [
        lax.dot_general(
            chosen[:, (1 + position) * functions : (2 + position) * functions],
            basis_in[position],
            plain,
            preferred_element_type=f32,
        )
        for position in range(4)
    ]
    for b in range(owned):
        target[pl.ds(b, 1), :] = own[pl.ds(b, 1), :] + correction[0:1, b * lanes : (b + 1) * lanes]
    take_margin(UPDATE, lambda position: None, lambda position: None)
    for position in range(4):
        target[pl.ds(owned + position * slots, 1), :] = update_in[position] + near[position][0:1]
    pressure_out[...] = target[pl.ds(0, owned), :]
    gather_faces(near_p, target)

    @pl.loop(0, owned, unroll=4)
    def _(b):
        row = pl.ds(b, 1)
        flux = trans[:, pl.ds(pl.multiple_of(b * lanes, lanes), lanes)] * (target[row, :] - near_p[b])
        outward, inward = jnp.maximum(flux, 0.0), jnp.minimum(flux, 0.0)
        adv[row, :] = jnp.sum(outward * conc[row, :] + inward * near_c[b], axis=0, keepdims=True)
        ext_b[row, :] = jnp.sum(outward, axis=0, keepdims=True)

    cell_rate = (ext_b[pl.ds(0, owned), :] + rate[...]) / volume[...]
    top_mine[...] = jnp.max(cell_rate, axis=0, keepdims=True)
    tops[0]()
    scaled = (rate[...] * (inject[...] - conc[...]) - adv[...]) / volume[...]

    for kind in range(5):
        for position, offset in enumerate(shift_offsets):
            @pl.when(inside(offset))
            def _():
                margin_copy(kind, position).wait_send()
    residuals[2]()
    values_all[2]()
    top_in[me] = top_mine[...]
    tops[1]()
    top = jnp.max(top_in[...], axis=0)
    time_step = courant / jnp.max(top, axis=1, keepdims=True)
    conc_out[...] = conc[...] + time_step * scaled
    tops[2]()


def hand_over(pressure, conc, pressure_out, conc_out, sem):
    copies = [
        pltpu.make_async_copy(pressure, pressure_out, sem.at[0]),
        pltpu.make_async_copy(conc, conc_out, sem.at[1]),
    ]
    for copy in copies:
        copy.start()
    for copy in copies:
        copy.wait()


def solution(mesh):
    wide_count, narrow_count = mesh.shape["wide"], mesh.shape["narrow"]

    def local(
        pressure,
        right_side,
        concentration,
        pore_volume,
        well_rate,
        inject_conc,
        transmissibility,
        face_neighbor,
        sub_matrix,
        sub_columns,
        send_blocks,
        send_counts,
        basis_weights,
        coarse_index,
        coarse_inverse,
    ):
        owned, lanes = pressure.shape
        extent = sub_matrix.shape[0]
        slots = send_blocks.shape[-1]
        faces = face_neighbor.shape[0]
        functions = coarse_index.shape[0]
        coarse_rows, coarse_width = coarse_inverse.shape
        devices = wide_count * narrow_count
        groups = coarse_width // lanes
        numbers = (face_neighbor, sub_columns.T, send_blocks, send_counts)
        index_row = coarse_index.reshape(1, functions)
        streamed = (
            pressure,
            right_side,
            concentration,
            pore_volume,
            well_rate,
            inject_conc,
            transmissibility,
            sub_matrix,
            basis_weights,
            coarse_inverse,
        )
        dma, vmem = pltpu.SemaphoreType.DMA, pltpu.VMEM
        field, ext = vmem((owned, lanes), f32), vmem((extent, lanes), f32)
        results = pl.pallas_call(
            functools.partial(kernel, wide_count, narrow_count),
            out_shape=(vmem((owned, lanes), f32), vmem((owned, lanes), f32)),
            in_specs=[pl.BlockSpec(memory_space=pltpu.HBM)] * 15,
            out_specs=[pl.BlockSpec(memory_space=pltpu.VMEM)] * 2,
            scratch_shapes=[pltpu.SMEM(value.shape, value.dtype) for value in numbers]
            + [vmem(value.shape, value.dtype) for value in (index_row,) + streamed]
            + [
                dma((16,)),
                vmem((2, 4, slots, lanes), f32),
                vmem((2, 4, slots, lanes), f32),
                vmem((4, slots, lanes), f32),
                vmem((4, slots, lanes), f32),
                vmem((4, functions, lanes), bf16),
                vmem((4, functions, lanes), bf16),
                vmem((4, 1, lanes), f32),
                vmem((4, 1, lanes), f32),
                dma((5, 4)),
                dma((5, 4)),
                field,
                ext,
                ext,
                ext,
                ext,
                vmem((4, extent, lanes), f32),
                vmem((5 * functions, devices), bf16),
                vmem((5 * functions, lanes), jnp.int32),
                vmem((wide_count, groups, lanes), f32),
                vmem((devices, groups, lanes), f32),
                vmem((devices, 1, coarse_rows), f32),
                vmem((1, coarse_rows), f32),
                vmem((1, lanes), f32),
                vmem((devices, 1, lanes), f32),
                dma((3,)),
                dma((3,)),
                vmem((owned, faces, lanes), f32),
                vmem((owned, faces, lanes), f32),
                ext,
                field,
                pltpu.SemaphoreType.REGULAR((8,)),
                ext,
                ext,
            ],
            compiler_params=pltpu.CompilerParams(
                collective_id=0, has_side_effects=True, vmem_limit_bytes=65400 << 10
            ),
            name="iteration",
        )(*numbers, index_row, *streamed)
        out = jax.ShapeDtypeStruct((owned, lanes), f32)
        return pl.pallas_call(
            hand_over,
            out_shape=(out, out),
            in_specs=[pl.BlockSpec(memory_space=pltpu.VMEM)] * 2,
            out_specs=[pl.BlockSpec(memory_space=pltpu.HBM)] * 2,
            scratch_shapes=[dma((2,))],
            compiler_params=pltpu.CompilerParams(vmem_limit_bytes=1 << 20),
            name="results",
        )(*results)

    split = ("wide", "narrow")
    return jax.shard_map(
        local,
        mesh=mesh,
        in_specs=(
            P(split, None),
            P(split, None),
            P(split, None),
            P(split, None),
            P(split, None),
            P(split, None),
            P(None, split),
            P(None, split),
            P(split, None, None, None),
            P(split, None),
            P(split, None, None),
            P(split, None),
            P(split, None),
            P(split),
            P(split, None),
        ),
        out_specs=(P(split, None), P(split, None)),
        check_vma=False,
    )
```

```python
import functools

import jax
import jax.numpy as jnp
from jax import lax
from jax.experimental import pallas as pl
from jax.experimental.pallas import tpu as pltpu
from jax.sharding import PartitionSpec as P

SWEEPS = 4
MATRIX_ROWS = 4

shift_offsets = (2, 1, -1, -2)
courant = 0.9
MESH = pl.DeviceIdType.MESH
f32, bf16 = jnp.float32, jnp.bfloat16
contract_last = (((1,), (1,)), ((), ()))
plain = (((1,), (0,)), ((), ()))
PRESSURE, RESIDUAL, EXTRAS, BASIS, UPDATE = range(5)


def rounded(value):
    return value.astype(bf16).astype(f32)


def kernel(
    wide_count,
    narrow_count,
    face_hbm,
    columns_hbm,
    blocks_hbm,
    counts_hbm,
    index_hbm,
    pressure_hbm,
    right_hbm,
    conc_hbm,
    volume_hbm,
    rate_hbm,
    inject_hbm,
    trans_hbm,
    matrix_hbm,
    basis_hbm,
    inverse_hbm,
    pressure_out,
    conc_out,
    face_neighbor,
    sub_columns,
    send_blocks,
    send_counts,
    index_row,
    pressure,
    right_side,
    conc,
    volume,
    rate,
    inject,
    trans,
    matrix,
    basis,
    inverse,
    load_sem,
    outbox,
    inbox,
    extras_out,
    extras_in,
    basis_out,
    basis_in,
    update_out,
    update_in,
    margin_send,
    margin_recv,
    own,
    ext_a,
    ext_b,
    target,
    diag,
    picked,
    row_of,
    lane_of,
    partial,
    residual_in,
    value_in,
    value_mine,
    top_mine,
    top_in,
    all_send,
    all_recv,
    near_p,
    near_c,
    ext_c,
    adv,
    grow,
    near_a,
    near_b,
):
    w, n = lax.axis_index("wide"), lax.axis_index("narrow")
    devices, me = wide_count * narrow_count, w * narrow_count + n
    owned, lanes = pressure.shape
    extent = ext_a.shape[0]
    slots = outbox.shape[2]
    faces = trans.shape[0]
    functions = index_row.shape[1]
    chunks = functions // lanes
    groups = partial.shape[1]
    coarse_rows, coarse_width = inverse.shape
    coarse_lines = wide_count * groups

    def wrapped(at, count):
        return jnp.where(at >= count, at - count, at)

    def inside(offset):
        return jnp.logical_and(w + offset >= 0, w + offset < wide_count)

    def others_narrow(body):
        for step in range(1, narrow_count):
            body(w, wrapped(n + step, narrow_count))

    def signal(sem, row, column):
        pl.semaphore_signal(sem, inc=1, device_id=(row, column), device_id_type=MESH)

    barrier = pltpu.get_barrier_semaphore()

    def meet(sem, offsets):
        for offset in offsets:
            @pl.when(inside(offset))
            def _():
                signal(sem, w + offset, n)

    def met(sem, offsets, more=0):
        pl.semaphore_wait(sem, more + sum(jnp.where(inside(offset), 1, 0) for offset in offsets))

    meet(barrier, shift_offsets)
    others_narrow(lambda row, column: signal(barrier, row, column))

    loads = {}

    def load(name, source, place):
        copy = pltpu.make_async_copy(source, place, load_sem.at[len(loads)])
        copy.start()
        loads[name] = copy

    def ready(*names):
        for name in names:
            loads[name].wait()

    rest = extent - owned
    load("pressure", pressure_hbm, pressure)
    load("blocks", blocks_hbm, send_blocks)
    load("counts", counts_hbm, send_counts)
    load("columns", columns_hbm, sub_columns)
    load("index", index_hbm, index_row)
    load("matrix", matrix_hbm.at[pl.ds(0, owned)], matrix.at[pl.ds(0, owned)])
    load("right", right_hbm, right_side)
    load("conc", conc_hbm, conc)
    load("basis", basis_hbm, basis)
    load("more", matrix_hbm.at[pl.ds(owned, rest)], matrix.at[pl.ds(owned, rest)])
    load("inverse", inverse_hbm, inverse)
    load("faces", face_hbm, face_neighbor)
    load("trans", trans_hbm, trans)
    load("volume", volume_hbm, volume)
    load("rate", rate_hbm, rate)
    load("inject", inject_hbm, inject)

    boxes = (
        lambda at: (outbox.at[0, at], inbox.at[0, at]),
        lambda at: (outbox.at[1, at], inbox.at[1, at]),
        lambda at: (extras_out.at[at], extras_in.at[at]),
        lambda at: (basis_out.at[at], basis_in.at[at]),
        lambda at: (update_out.at[at], update_in.at[at]),
    )

    def margin_copy(kind, position):
        source, place = boxes[kind](position)
        return pltpu.make_async_remote_copy(
            src_ref=source,
            dst_ref=place,
            send_sem=margin_send.at[kind, position],
            recv_sem=margin_recv.at[kind, position],
            device_id=(w + shift_offsets[position], n),
            device_id_type=MESH,
        )

    slot_id = lax.broadcasted_iota(jnp.int32, (slots, lanes), 0)

    def pack(turn, rows):
        for position in range(4):
            for t in range(slots):
                outbox[turn, position, pl.ds(t, 1), :] = rows[pl.ds(send_blocks[0, position, t], 1), :]
            filled = outbox[turn, position]
            outbox[turn, position] = jnp.where(slot_id < send_counts[0, position], filled, 0.0)

    def send_margin(kind):
        for position, offset in enumerate(shift_offsets):
            @pl.when(inside(offset))
            def _():
                margin_copy(kind, position).start()

    def take_margin(kind, use, nothing):
        for position, offset in enumerate(shift_offsets):
            @pl.when(inside(-offset))
            def _():
                margin_copy(kind, position).wait_recv()
                use(position)

            @pl.when(jnp.logical_not(inside(-offset)))
            def _():
                nothing(position)

    def take_rows(turn, place):
        def use(position):
            place[pl.ds(owned + position * slots, slots), :] = inbox[turn, position]

        def nothing(position):
            place[pl.ds(owned + position * slots, slots), :] = jnp.zeros((slots, lanes), f32)

        take_margin(turn, use, nothing)

    def exchange(turn, send_from, land_in):
        def start():
            def send(row, column):
                pltpu.make_async_remote_copy(
                    src_ref=send_from(row),
                    dst_ref=land_in.at[me],
                    send_sem=all_send.at[turn],
                    recv_sem=all_recv.at[turn],
                    device_id=(row, column),
                    device_id_type=MESH,
                ).start()

            columns = [n] + [wrapped(n + step, narrow_count) for step in range(1, narrow_count)]

            @pl.loop(1, wide_count, unroll=wide_count - 1 if wide_count <= 8 else 1)
            def _(step):
                row = wrapped(w + step, wide_count)
                for column in columns:
                    send(row, column)

            others_narrow(send)

        others = land_in.at[pl.ds(0, devices - 1)]
        every = pltpu.make_async_remote_copy(
            src_ref=others,
            dst_ref=others,
            send_sem=all_send.at[turn],
            recv_sem=all_recv.at[turn],
            device_id=(wrapped(w + 1, wide_count), n),
            device_id_type=MESH,
        )
        return start, every.wait_recv, every.wait_send

    residuals = exchange(0, lambda row: partial.at[row], residual_in)
    values_all = exchange(1, lambda row: value_mine, value_in)
    tops = exchange(2, lambda row: top_mine, top_in)

    ready("pressure", "blocks", "counts")
    own[...] = rounded(pressure[...])
    pack(0, own)
    met(barrier, shift_offsets, narrow_count - 1)
    send_margin(PRESSURE)

    radius, rounds = 2, []
    while radius < wide_count - 1:
        rounds.append((radius, -radius))
        radius *= 2
    if rounds:
        meet(grow.at[0], rounds[0])

    ready("index")
    power = coarse_rows.bit_length() - 1

    def spread_index(part, line, place):
        tall = jnp.broadcast_to(line, (lanes, lanes)).T.astype(jnp.int32)
        rows = pl.ds(part * lanes, lanes)
        line_of = jnp.right_shift(tall, power)
        wide_id = lax.broadcasted_iota(jnp.int32, (lanes, devices), 1)
        row_of[rows, :] = jnp.where(line_of[:, :1] == wide_id, 1.0, 0.0).astype(bf16)
        lane_of[rows, :] = jnp.bitwise_and(tall, coarse_rows - 1)
        return tall

    number = index_row[...]
    number_f = number.astype(f32)
    tall_parts = [spread_index(c, number_f[:, c * lanes : (c + 1) * lanes], None) for c in range(chunks)]
    lane_id = lax.broadcasted_iota(jnp.int32, (functions, lanes), 1)
    line_hot = jnp.where(
        jnp.right_shift(number, 7) == lax.broadcasted_iota(jnp.int32, (coarse_lines, functions), 0), 1.0, 0.0
    ).astype(bf16)

    def next_round(at):
        met(grow.at[at], rounds[at])
        if at + 1 < len(rounds):
            meet(grow.at[at + 1], rounds[at + 1])

    if rounds:
        next_round(0)

    ready("conc", "basis")
    for position in range(4):
        block = send_blocks[0, position, 0]
        extras_out[position, pl.ds(0, 1), :] = conc[pl.ds(block, 1), :]
        for c in range(chunks):
            extras_out[position, pl.ds(1 + c, 1), :] = number_f[:, c * lanes : (c + 1) * lanes]
        extras_out[position, pl.ds(1 + chunks, slots - 1 - chunks), :] = jnp.zeros((slots - 1 - chunks, lanes), f32)
        basis_out[position] = basis[:, pl.ds(block * lanes, lanes)]
    send_margin(EXTRAS)
    send_margin(BASIS)

    ready("matrix")
    eye = lax.broadcasted_iota(jnp.int32, (lanes, lanes), 0) == lax.broadcasted_iota(jnp.int32, (lanes, lanes), 1)

    def diagonals(start, stop):
        @pl.loop(start, stop, unroll=4)
        def _(row):
            block = matrix[row, 0].astype(f32)
            diag[pl.ds(row, 1), :] = jnp.sum(jnp.where(eye, block, 0.0), axis=0, keepdims=True)

    for at in range(1, len(rounds)):
        next_round(at)
    last = grow.at[len(rounds)]
    others_narrow(lambda row, column: signal(last, row, column))
    ready("columns", "right")

    sub_id = lax.broadcasted_iota(jnp.int32, (8, lanes), 0)

    def dense(row, columns, vector):
        terms = [matrix[row, k].astype(f32) * vector[pl.ds(column, 1), :] for k, column in enumerate(columns)]
        total = terms[0]
        for term in terms[1:]:
            total += term
        return jnp.sum(total.T, axis=0, keepdims=True)

    def product(group, vector):
        base = pl.multiple_of(group * 8, 8)
        for i in range(MATRIX_ROWS):
            for k in range(4):
                picked[k, pl.ds(base + i, 1), :] = vector[pl.ds(sub_columns[k, base + i], 1), :]
        left = jnp.concatenate([picked[k, pl.ds(base, 8), :].astype(bf16) for k in range(4)], axis=1)
        total = jnp.zeros((8, lanes), f32)
        for i in range(0, MATRIX_ROWS, 2):
            pair = matrix[pl.ds(base + i, 2)]
            blocks = jnp.concatenate([pair[:, k].reshape(2 * lanes, lanes) for k in range(4)], axis=1)
            made = lax.dot_general(left, blocks, contract_last, preferred_element_type=f32)
            total = jnp.where(sub_id == i, made[:, :lanes], total)
            total = jnp.where(sub_id == i + 1, made[:, lanes:], total)
        for i in range(MATRIX_ROWS, 8):
            row = base + i
            total = jnp.where(sub_id == i, dense(row, [sub_columns[k, row] for k in range(4)], vector), total)
        return total

    def groups_of(count, body, unroll=4):
        @pl.loop(0, count // 8, unroll=unroll)
        def _(group):
            body(group, pl.ds(pl.multiple_of(group * 8, 8), 8))

    ext_a[pl.ds(0, owned), :] = own[...]
    take_rows(PRESSURE, ext_a)

    def residual_group(group, rows):
        own[rows, :] = rounded(right_side[rows, :] - product(group, ext_a))

    groups_of(owned, residual_group, 2)
    pack(1, own)
    send_margin(RESIDUAL)

    dense_from = owned - owned // 2
    flat = jnp.concatenate([own[pl.ds(b, 1), :] for b in range(dense_from)], axis=1)
    flat = jnp.broadcast_to(flat, (8, flat.shape[1])).astype(bf16)
    tall_part = jnp.zeros((functions, lanes), f32)
    for b in range(dense_from, owned):
        tall_part += basis[:, b * lanes : (b + 1) * lanes].astype(f32) * own[pl.ds(b, 1), :]
    local_coarse = lax.dot_general(flat, basis[:, : dense_from * lanes], contract_last, preferred_element_type=f32)[0:1, :]
    tall_coarse = jnp.concatenate(
        [jnp.broadcast_to(local_coarse[:, c * lanes : (c + 1) * lanes], (lanes, lanes)).T for c in range(chunks)], axis=0
    )
    tall_coarse += jnp.sum(tall_part, axis=1, keepdims=True)
    tall_index = jnp.concatenate(tall_parts, axis=0)
    placed = jnp.where(jnp.bitwise_and(tall_index, lanes - 1) == lane_id, tall_coarse, 0.0)
    high = placed.astype(bf16)
    left_over = placed - high.astype(f32)
    middle = left_over.astype(bf16)
    low = (left_over - middle.astype(f32)).astype(bf16)
    spread = lax.dot_general(
        line_hot, jnp.concatenate([high, middle, low], axis=1), plain, preferred_element_type=f32
    )
    spread = spread[:, :lanes] + spread[:, lanes : 2 * lanes] + spread[:, 2 * lanes :]
    for block in range(wide_count):
        partial[block] = spread[block * groups : (block + 1) * groups]
    pl.semaphore_wait(last, narrow_count - 1)
    residuals[0]()

    ready("more")
    diagonals(0, extent)
    target[pl.ds(0, owned), :] = own[...]

    def use_extras(position):
        ext_c[pl.ds(owned + position * slots, slots), :] = extras_in[position]

    def no_extras(position):
        ext_c[pl.ds(owned + position * slots, slots), :] = jnp.zeros((slots, lanes), f32)
        basis_in[position] = jnp.zeros((functions, lanes), bf16)
        update_in[position] = jnp.zeros((1, lanes), f32)

    take_rows(RESIDUAL, target)
    ext_a[...] = target[...] / diag[...]
    near_a[...] = rounded(ext_a[...])

    def sweep(count, old, old_near, new, new_near):
        def body(group, rows):
            fresh = old[rows, :] + (target[rows, :] - product(group, old_near)) / diag[rows, :]
            new[rows, :] = fresh
            if new_near is not None:
                new_near[rows, :] = rounded(fresh)

        groups_of(count, body, 4 if new_near is not None else 2)

    sweep(extent, ext_a, near_a, ext_b, near_b)
    sweep(extent, ext_b, near_b, ext_a, near_a)

    ready("inverse")
    residual_in[me] = partial[w]
    residuals[1]()
    block_sum = jnp.sum(residual_in[...], axis=0)
    weighed = inverse[:, :lanes] * block_sum[0:1]
    for c in range(1, groups):
        weighed += inverse[:, c * lanes : (c + 1) * lanes] * block_sum[c : c + 1]
    value_mine[...] = rounded(jnp.sum(weighed.T, axis=0, keepdims=True))
    value_in[me] = value_mine[...]
    values_all[0]()

    for position in range(4):
        block = send_blocks[0, position, 0]
        row = pl.ds(block, 1)
        made = dense(block, [sub_columns[k, block] for k in range(4)], near_a)
        update_out[position] = pressure[row, :] + (ext_a[row, :] + (target[row, :] - made) / diag[row, :])
    send_margin(UPDATE)

    sweep(owned, ext_a, near_a, ext_b, None)
    own[...] = pressure[...] + ext_b[pl.ds(0, owned), :]

    ext_c[pl.ds(0, owned), :] = conc[...]
    take_margin(EXTRAS, use_extras, no_extras)
    for position in range(4):
        for c in range(chunks):
            line = ext_c[pl.ds(owned + position * slots + 1 + c, 1), :]
            spread_index((1 + position) * chunks + c, line, None)

    def gather_faces(place, field):
        @pl.loop(0, owned, unroll=4)
        def _(b):
            for f in range(faces):
                place[b, pl.ds(f, 1), :] = field[pl.ds(face_neighbor[f, b], 1), :]

    ready("faces")
    gather_faces(near_c, ext_c)
    ready("trans", "volume", "rate", "inject")
    take_margin(BASIS, lambda position: None, lambda position: None)
    target[pl.ds(owned, extent - owned), :] = jnp.zeros((extent - owned, lanes), f32)

    values_all[1]()
    coarse = value_in[...].reshape(devices, coarse_rows).astype(bf16)
    lined = lax.dot_general(row_of[...], coarse, plain, preferred_element_type=f32)
    value_lane = lax.broadcasted_iota(jnp.int32, lined.shape, 1)
    lined = jnp.where(lane_of[:, :coarse_rows] == value_lane, lined, 0.0).astype(bf16)
    chosen = lax.dot_general(
        jnp.ones((8, coarse_rows), bf16), lined, contract_last, preferred_element_type=f32
    ).astype(bf16)
    correction = lax.dot_general(chosen[:, :functions], basis[...], plain, preferred_element_type=f32)
    near = [
        lax.dot_general(
            chosen[:, (1 + position) * functions : (2 + position) * functions],
            basis_in[position],
            plain,
            preferred_element_type=f32,
        )
        for position in range(4)
    ]
    for b in range(owned):
        target[pl.ds(b, 1), :] = own[pl.ds(b, 1), :] + correction[0:1, b * lanes : (b + 1) * lanes]
    take_margin(UPDATE, lambda position: None, lambda position: None)
    for position in range(4):
        target[pl.ds(owned + position * slots, 1), :] = update_in[position] + near[position][0:1]
    pressure_out[...] = target[pl.ds(0, owned), :]
    gather_faces(near_p, target)

    @pl.loop(0, owned, unroll=4)
    def _(b):
        row = pl.ds(b, 1)
        flux = trans[:, pl.ds(pl.multiple_of(b * lanes, lanes), lanes)] * (target[row, :] - near_p[b])
        outward, inward = jnp.maximum(flux, 0.0), jnp.minimum(flux, 0.0)
        adv[row, :] = jnp.sum(outward * conc[row, :] + inward * near_c[b], axis=0, keepdims=True)
        ext_b[row, :] = jnp.sum(outward, axis=0, keepdims=True)

    cell_rate = (ext_b[pl.ds(0, owned), :] + rate[...]) / volume[...]
    top_mine[...] = jnp.max(cell_rate, axis=0, keepdims=True)
    tops[0]()
    scaled = (rate[...] * (inject[...] - conc[...]) - adv[...]) / volume[...]

    for kind in range(5):
        for position, offset in enumerate(shift_offsets):
            @pl.when(inside(offset))
            def _():
                margin_copy(kind, position).wait_send()
    residuals[2]()
    values_all[2]()
    top_in[me] = top_mine[...]
    tops[1]()
    top = jnp.max(top_in[...], axis=0)
    time_step = courant / jnp.max(top, axis=1, keepdims=True)
    conc_out[...] = conc[...] + time_step * scaled
    tops[2]()


def hand_over(pressure, conc, pressure_out, conc_out, sem):
    copies = [
        pltpu.make_async_copy(pressure, pressure_out, sem.at[0]),
        pltpu.make_async_copy(conc, conc_out, sem.at[1]),
    ]
    for copy in copies:
        copy.start()
    for copy in copies:
        copy.wait()


def solution(mesh):
    wide_count, narrow_count = mesh.shape["wide"], mesh.shape["narrow"]

    def local(
        pressure,
        right_side,
        concentration,
        pore_volume,
        well_rate,
        inject_conc,
        transmissibility,
        face_neighbor,
        sub_matrix,
        sub_columns,
        send_blocks,
        send_counts,
        basis_weights,
        coarse_index,
        coarse_inverse,
    ):
        owned, lanes = pressure.shape
        extent = sub_matrix.shape[0]
        slots = send_blocks.shape[-1]
        faces = face_neighbor.shape[0]
        functions = coarse_index.shape[0]
        coarse_rows, coarse_width = coarse_inverse.shape
        devices = wide_count * narrow_count
        groups = coarse_width // lanes
        numbers = (face_neighbor, sub_columns.T, send_blocks, send_counts)
        index_row = coarse_index.reshape(1, functions)
        streamed = (
            pressure,
            right_side,
            concentration,
            pore_volume,
            well_rate,
            inject_conc,
            transmissibility,
            sub_matrix,
            basis_weights,
            coarse_inverse,
        )
        dma, vmem = pltpu.SemaphoreType.DMA, pltpu.VMEM
        field, ext = vmem((owned, lanes), f32), vmem((extent, lanes), f32)
        results = pl.pallas_call(
            functools.partial(kernel, wide_count, narrow_count),
            out_shape=(vmem((owned, lanes), f32), vmem((owned, lanes), f32)),
            in_specs=[pl.BlockSpec(memory_space=pltpu.HBM)] * 15,
            out_specs=[pl.BlockSpec(memory_space=pltpu.VMEM)] * 2,
            scratch_shapes=[pltpu.SMEM(value.shape, value.dtype) for value in numbers]
            + [vmem(value.shape, value.dtype) for value in (index_row,) + streamed]
            + [
                dma((16,)),
                vmem((2, 4, slots, lanes), f32),
                vmem((2, 4, slots, lanes), f32),
                vmem((4, slots, lanes), f32),
                vmem((4, slots, lanes), f32),
                vmem((4, functions, lanes), bf16),
                vmem((4, functions, lanes), bf16),
                vmem((4, 1, lanes), f32),
                vmem((4, 1, lanes), f32),
                dma((5, 4)),
                dma((5, 4)),
                field,
                ext,
                ext,
                ext,
                ext,
                vmem((4, extent, lanes), f32),
                vmem((5 * functions, devices), bf16),
                vmem((5 * functions, lanes), jnp.int32),
                vmem((wide_count, groups, lanes), f32),
                vmem((devices, groups, lanes), f32),
                vmem((devices, 1, coarse_rows), f32),
                vmem((1, coarse_rows), f32),
                vmem((1, lanes), f32),
                vmem((devices, 1, lanes), f32),
                dma((3,)),
                dma((3,)),
                vmem((owned, faces, lanes), f32),
                vmem((owned, faces, lanes), f32),
                ext,
                field,
                pltpu.SemaphoreType.REGULAR((8,)),
                ext,
                ext,
            ],
            compiler_params=pltpu.CompilerParams(
                collective_id=0, has_side_effects=True, vmem_limit_bytes=65400 << 10
            ),
            name="iteration",
        )(*numbers, index_row, *streamed)
        out = jax.ShapeDtypeStruct((owned, lanes), f32)
        return pl.pallas_call(
            hand_over,
            out_shape=(out, out),
            in_specs=[pl.BlockSpec(memory_space=pltpu.VMEM)] * 2,
            out_specs=[pl.BlockSpec(memory_space=pltpu.HBM)] * 2,
            scratch_shapes=[dma((2,))],
            compiler_params=pltpu.CompilerParams(vmem_limit_bytes=1 << 20),
            name="results",
        )(*results)

    split = ("wide", "narrow")
    return jax.shard_map(
        local,
        mesh=mesh,
        in_specs=(
            P(split, None),
            P(split, None),
            P(split, None),
            P(split, None),
            P(split, None),
            P(split, None),
            P(None, split),
            P(None, split),
            P(split, None, None, None),
            P(split, None),
            P(split, None, None),
            P(split, None),
            P(split, None),
            P(split),
            P(split, None),
        ),
        out_specs=(P(split, None), P(split, None)),
        check_vma=False,
    )
```
